32 devices in a mesh: dp: 4 (over y, core), wide: 8 (over z, x).
Axes of the slice: x: 2, y: 2, z: 4, core: 2. Of those that a mesh axis runs over, the one named last changes fastest.
Arguments:
- frames: bfloat16 [4, 2, 16, 64, 512], P('dp', None, 'wide'), may hold values from -6 to 6
- conv_weight: bfloat16 [3, 512, 512], replicated, may hold values from -0.15625 to 0.15625
- embed_weight: bfloat16 [512, 1536], replicated, may hold values from -0.25 to 0.25
- query_weight: bfloat16 [1536, 1536], P('wide'), may hold values from -3 to 3
- key_weight: bfloat16 [1536, 1536], P('wide'), may hold values from -3 to 3
- value_weight: bfloat16 [1536, 1536], P('wide'), may hold values from -0.15625 to 0.15625
- output_weight: bfloat16 [1536, 1536], P('wide'), may hold values from -0.15625 to 0.15625
- out_grad: bfloat16 [4, 4, 16, 64, 1536], P('dp', None, 'wide'), may hold values from -0.119628906 to 0.119628906
- bucket_owner: int32 [16], replicated, may hold values from 0 to 3, as said below
- clip_bucket: int32 [4, 2], replicated, may hold values from 0 to 15, as said below
- clip_frames: int32 [4, 2], replicated, may hold values from 4 to 16, as said below
- clip_grid: int32 [4, 2, 2], replicated, may hold values from 2 to 32, as said below
Outputs:
- block_out: bfloat16 [4, 4, 16, 64, 1536], P('dp', None, 'wide')
- grad_query: float32 [1536, 1536], P('wide')
- grad_key: float32 [1536, 1536], P('wide')
- grad_value: float32 [1536, 1536], P('wide')
- grad_output: float32 [1536, 1536], P('wide')
The draws below stay inside these ranges and needn't reach their ends.
Inputs may be any that keep to these rules, and one draw needn't show every extreme that they name: `bucket_owner`: each owner has exactly 4 buckets. `clip_bucket`: the 2 clips of one group have buckets of different owners; some owner has a clip of every group. `clip_frames`: some clip has all 16 frames. `clip_grid`: the product of a clip's two entries is at most 64, and equals it for some clip.
All inputs are finite; a program needn't handle non-finite values.
Results may differ from the reference program's by a relative error of at most 0.025.
Values may be sent and summed in bfloat16 or wider, within the bound.
A program may use at most 128 MiB of HBM per device.

```python
import math
import jax
import jax.numpy as jnp
from jax import lax

D = 1536
HEADS = 12
HEAD_DIM = 128
CHANNELS = 512
SITES = 64
FR_DEV = 2
CLIPS = 2
OWNER_BUCKETS = 4
TIME = 16
BUCKETS = 16
N_DP = 4
N_WIDE = 8


def bucket_plan(key):
    base = jax.random.fold_in(key, 11)
    order = jax.random.permutation(jax.random.fold_in(base, 1), BUCKETS)
    owners = order % N_DP
    inverse = jnp.argsort(order)
    last_code = order[BUCKETS - 1]
    anchor = last_code % N_DP
    last_pick = last_code // N_DP

    def one_group(group):
        group_key = jax.random.fold_in(base, 100 + group)
        others = (anchor + 1 + jax.random.permutation(jax.random.fold_in(group_key, 1), N_DP - 1)) % N_DP
        chosen = jnp.concatenate([anchor[None], others])[:CLIPS]
        picked = jax.random.randint(jax.random.fold_in(group_key, 3), (CLIPS,), 0, OWNER_BUCKETS)
        first_pick = jnp.where(group == 0, last_pick, picked[0])
        picked = jnp.concatenate([first_pick[None], picked[1:]])
        buckets = inverse[chosen + N_DP * picked]
        return jax.random.permutation(jax.random.fold_in(group_key, 2), buckets)
    buckets = jax.vmap(one_group)(jnp.arange(N_DP))
    return (owners.astype(jnp.int32), buckets.astype(jnp.int32))


def draw_bucket_owner(key, part):
    return bucket_plan(key)[0]


def draw_clip_bucket(key, part):
    return bucket_plan(key)[1]


def draw_clip_frames(key, part):
    base = jax.random.fold_in(key, 31)
    counts = jax.random.randint(jax.random.fold_in(base, 1), (N_DP * CLIPS,), TIME // 4, TIME + 1)
    chosen = jax.random.randint(jax.random.fold_in(base, 2), (), 0, N_DP * CLIPS)
    counts = jnp.where(jnp.arange(N_DP * CLIPS) == chosen, TIME, counts)
    return counts.reshape(N_DP, CLIPS).astype(jnp.int32)


def draw_clip_grid(key, part):
    base = jax.random.fold_in(key, 37)
    grid_rows = jax.random.randint(jax.random.fold_in(base, 1), (N_DP * CLIPS,), 2, 9)
    trimmed = jax.random.randint(jax.random.fold_in(base, 2), (N_DP * CLIPS,), 0, 2)
    order = jax.random.permutation(jax.random.fold_in(base, 3), N_DP * CLIPS)
    position = jnp.arange(N_DP * CLIPS)
    full_mark = position == order[0]
    tall_mark = position == order[1]
    narrow_mark = position == order[2]
    grid_rows = jnp.where(full_mark, 8, grid_rows)
    trimmed = jnp.where(full_mark, 0, trimmed)
    grid_rows = jnp.where(tall_mark, 2, grid_rows)
    trimmed = jnp.where(tall_mark, 0, trimmed)
    grid_rows = jnp.where(narrow_mark, 8, grid_rows)
    trimmed = jnp.where(narrow_mark, 1, trimmed)
    grid_cols = SITES // grid_rows - trimmed
    return jnp.stack([grid_rows, grid_cols], axis=-1).reshape(N_DP, CLIPS, 2).astype(jnp.int32)


def query_key_base(key):
    base = jax.random.fold_in(key, 47)
    shape = (D, HEADS * HEAD_DIM)
    shared = jnp.clip(jax.random.normal(jax.random.fold_in(base, 1), shape, jnp.float32), -4.0, 4.0)
    other = jnp.clip(jax.random.normal(jax.random.fold_in(base, 2), shape, jnp.float32), -4.0, 4.0)
    return (shared, other)


def draw_query_weight(key, part):
    shared, other = query_key_base(key)
    values = shared
    return (values / math.sqrt(D)).astype(jnp.bfloat16)


def draw_key_weight(key, part):
    shared, other = query_key_base(key)
    values = other
    return (values / math.sqrt(D)).astype(jnp.bfloat16)


def block_levels(own_key, dims, pieces, low, high):
    loudness = 1.0
    for dim, parts in pieces:
        heights = jax.random.uniform(jax.random.fold_in(jax.random.fold_in(own_key, 6), dim), (parts,), jnp.float32, low / len(pieces), high / len(pieces))
        loudness = loudness * jnp.repeat(jnp.exp(heights), dims[dim] // parts).reshape((-1,) + (1,) * (len(dims) - 1 - dim))
    return loudness


def gaussian(rng, shape, scale, bound, cuts=(), kind=jnp.bfloat16):
    result = jax.random.normal(rng, shape, jnp.float32) * scale
    if len(cuts) > 0:
        result = block_levels(rng, shape, cuts, -0.22, 0.18) * result
    return jnp.clip(result, min=-bound, max=bound).astype(kind)


def setup_inputs(seed: int = 0) -> dict:
    key_list = jax.random.split(jax.random.key(seed), 13)
    frames = gaussian(key_list[0], (N_DP, CLIPS, TIME, SITES, CHANNELS), 1.0, 6.0, ((0, 4), (2, 8)))
    conv_weight = gaussian(key_list[1], (3, CHANNELS, CHANNELS), (3 * CHANNELS) ** -0.5, 0.15625)
    embed_weight = gaussian(key_list[2], (CHANNELS, D), CHANNELS ** -0.5, 0.25)
    query_weight = draw_query_weight(jax.random.fold_in(key_list[12], 71), 0)
    key_weight = draw_key_weight(jax.random.fold_in(key_list[12], 71), 0)
    value_weight = gaussian(key_list[5], (D, HEADS * HEAD_DIM), D ** -0.5, 0.15625, ((0, 8),))
    output_weight = gaussian(key_list[6], (HEADS * HEAD_DIM, D), (HEADS * HEAD_DIM) ** -0.5, 0.15625, ((0, 8),))
    out_grad = gaussian(key_list[7], (N_DP, N_DP, TIME, SITES, D), 0.02, 0.119628906, ((0, 4), (2, 8)))
    bucket_owner = draw_bucket_owner(jax.random.fold_in(key_list[12], 71), 0)
    clip_bucket = draw_clip_bucket(jax.random.fold_in(key_list[12], 71), 0)
    clip_frames = draw_clip_frames(jax.random.fold_in(key_list[12], 71), 0)
    clip_grid = draw_clip_grid(jax.random.fold_in(key_list[12], 71), 0)
    return {"frames": frames, "conv_weight": conv_weight, "embed_weight": embed_weight, "query_weight": query_weight, "key_weight": key_weight, "value_weight": value_weight, "output_weight": output_weight, "out_grad": out_grad, "bucket_owner": bucket_owner, "clip_bucket": clip_bucket, "clip_frames": clip_frames, "clip_grid": clip_grid}


EPS = 1e-06
masked_score = -1e+30

def widen(array):
    return lax.optimization_barrier(array).astype(jnp.float32)

def layer_norm(values):
    floats = values.astype(jnp.float32)
    center = floats - lax.optimization_barrier(jnp.mean(floats, axis=-1, keepdims=True))
    spread = lax.optimization_barrier(jnp.mean(center * center, axis=-1, keepdims=True))
    return (center * lax.rsqrt(spread + EPS)).astype(jnp.bfloat16)

def reference(frames, conv_weight, embed_weight, query_weight, key_weight, value_weight, output_weight, out_grad, bucket_owner, clip_bucket, clip_frames, clip_grid):
    scale = 1.0 / math.sqrt(HEAD_DIM)
    active = widen(jax.nn.silu(frames.astype(jnp.float32)).astype(jnp.bfloat16))
    summed = frames.astype(jnp.float32)
    for offset in range(3):
        moved = jnp.pad(active, ((0, 0), (0, 0), (offset, 0), (0, 0), (0, 0)))[:, :, :TIME]
        summed = summed + jnp.einsum('gctsa,ab->gctsb', moved, conv_weight[offset].astype(jnp.float32))
    encoded = summed.astype(jnp.bfloat16)
    embedded = jnp.einsum('gctsa,ad->gctsd', widen(encoded), embed_weight.astype(jnp.float32)).astype(jnp.bfloat16)
    owners = bucket_owner[clip_bucket]
    group_index = jnp.arange(N_DP, dtype=jnp.int32)
    table = (owners[None, :, :] == group_index[:, None, None]).astype(jnp.int32)
    grouped = jnp.einsum('ogc,gctsd->ogtsd', table.astype(jnp.float32), widen(embedded)).astype(jnp.bfloat16)
    live_frames = lax.optimization_barrier(jnp.sum(table * clip_frames[None], axis=-1))
    grid_tokens = clip_grid[..., 0] * clip_grid[..., 1]
    live_tokens = lax.optimization_barrier(jnp.sum(table * grid_tokens[None], axis=-1))
    key_tokens = jnp.where(live_tokens > 0, live_tokens, SITES)
    time_pos = jnp.arange(TIME, dtype=jnp.int32)
    site_pos = jnp.arange(SITES, dtype=jnp.int32)
    live = (time_pos[None, None, :, None] < live_frames[:, :, None, None]) & (site_pos[None, None, None, :] < live_tokens[:, :, None, None])
    normed = layer_norm(widen(grouped))
    head_shape = (N_DP, N_DP, TIME, SITES, HEADS, HEAD_DIM)
    query = jnp.einsum('ogtsd,de->ogtse', widen(normed), query_weight.astype(jnp.float32)).astype(jnp.bfloat16)
    keys = jnp.einsum('ogtsd,de->ogtse', widen(normed), key_weight.astype(jnp.float32)).astype(jnp.bfloat16)
    values = jnp.einsum('ogtsd,de->ogtse', widen(normed), value_weight.astype(jnp.float32)).astype(jnp.bfloat16)
    query_heads = query.reshape(head_shape)
    key_heads = keys.reshape(head_shape)
    value_heads = values.reshape(head_shape)
    scores = jnp.einsum('ogtshd,ogtuhd->ogthsu', widen(query_heads), widen(key_heads)) * scale
    key_mask = site_pos[None, None, :] < key_tokens[:, :, None]
    scores = jnp.where(key_mask[:, :, None, None, None, :], scores, masked_score)
    top = lax.optimization_barrier(jnp.max(scores, axis=-1, keepdims=True))
    weights = jnp.exp(scores - top)
    probs = weights / lax.optimization_barrier(jnp.sum(weights, axis=-1, keepdims=True))
    probs_low = probs.astype(jnp.bfloat16)
    attended = jnp.einsum('ogthsu,ogtuhd->ogtshd', widen(probs_low), widen(value_heads)).astype(jnp.bfloat16)
    attended = attended.reshape(N_DP, N_DP, TIME, SITES, D)
    projected = jnp.einsum('ogtsk,kd->ogtsd', widen(attended), output_weight.astype(jnp.float32))
    block = (widen(grouped) + projected).astype(jnp.bfloat16)
    block_out = jnp.where(live[..., None], block, jnp.zeros((), jnp.bfloat16))
    upstream = jnp.where(live[..., None], out_grad, jnp.zeros((), jnp.bfloat16))
    d_attended = jnp.einsum('ogtsd,kd->ogtsk', upstream.astype(jnp.float32), output_weight.astype(jnp.float32)).astype(jnp.bfloat16)
    d_att_heads = d_attended.reshape(head_shape)
    d_probs = jnp.einsum('ogtshd,ogtuhd->ogthsu', widen(d_att_heads), widen(value_heads))
    inner = lax.optimization_barrier(jnp.sum(probs * d_probs, axis=-1, keepdims=True))
    d_scores = (probs * (d_probs - inner) * scale).astype(jnp.bfloat16)
    d_query = jnp.einsum('ogthsu,ogtuhd->ogtshd', widen(d_scores), widen(key_heads)).astype(jnp.bfloat16).reshape(N_DP, N_DP, TIME, SITES, D)
    d_keys = jnp.einsum('ogthsu,ogtshd->ogtuhd', widen(d_scores), widen(query_heads)).astype(jnp.bfloat16).reshape(N_DP, N_DP, TIME, SITES, D)
    d_values = jnp.einsum('ogthsu,ogtshd->ogtuhd', widen(probs_low), widen(d_att_heads)).astype(jnp.bfloat16).reshape(N_DP, N_DP, TIME, SITES, D)
    pairs = ((normed, d_query), (normed, d_keys), (normed, d_values), (attended, upstream))
    zero_index = jnp.zeros((), jnp.int32)

    def add_block(running, index):
        owner_pos = index // N_WIDE
        slab_pos = index % N_WIDE * FR_DEV
        starts = (owner_pos, zero_index, slab_pos, zero_index, zero_index)
        updated = []
        for accum, pair in zip(running, pairs):
            left_rows = lax.dynamic_slice(pair[0], starts, (1, N_DP, FR_DEV, SITES, D)).reshape(-1, D)
            right_rows = lax.dynamic_slice(pair[1], starts, (1, N_DP, FR_DEV, SITES, D)).reshape(-1, D)
            term = jnp.dot(left_rows.T, right_rows, preferred_element_type=jnp.float32)
            updated.append(accum + widen(term.astype(jnp.bfloat16)))
        return (tuple(updated), None)
    empty = jnp.zeros((D, D), jnp.float32)
    totals, unused = lax.scan(add_block, (empty, empty, empty, empty), jnp.arange(N_DP * N_WIDE, dtype=jnp.int32))
    return (block_out, totals[0], totals[1], totals[2], totals[3])
```

```python
import functools
import math

import jax
import jax.numpy as jnp
from jax import lax
from jax.experimental import pallas as pl
from jax.experimental.pallas import tpu as pltpu
from jax.sharding import PartitionSpec as P

HEAD_DIM = 128
MESH = pl.DeviceIdType.MESH
EPS = 1e-06
masked_score = -1e30
F32, BF16 = jnp.float32, jnp.bfloat16


def remote(src, dst, send, recv, peer):
    return pltpu.make_async_remote_copy(
        src_ref=src, dst_ref=dst, send_sem=send, recv_sem=recv, device_id=peer, device_id_type=MESH
    )


def span(start, size):
    return pl.ds(pl.multiple_of(start, 128 if size % 128 == 0 else 16), size)


def both(*conds):
    out = None
    for cond in conds:
        if cond is not None:
            out = cond if out is None else jnp.logical_and(out, cond)
    return out


def guarded(cond, action):
    if cond is None:
        action()
    else:
        pl.when(cond)(action)


def kernel(n_wide, clips, fr, sites, scale, *refs):
    frames, conv_in, embed_in, wq, wk, wv, wo, og_in, pick, klim = refs[:10]
    block_out, fin_q, fin_k, fin_v, fin_o = refs[10:15]
    (
        fbuf, conv, embed, weights, out_w, enc, tokens, normed, normed_t, og, upst, qkv, datt, att, att_t,
        dqkv, probs, px_out, px_in, y_in, term_out, term_in, keep, from_low, from_high,
    ) = refs[15:40]
    (
        loc, halo, xw, xo, zs, zr, bs, br, es, er, gs, gr, us, ur, ps, pr, ys, yr, cs, cr, rs, rl, rh,
        a_s, a_r, b_s, b_r, f_s, f_r,
    ) = refs[40:]
    levels = n_wide // 2
    in_w = (wq, wk, wv)
    fins = (fin_q, fin_k, fin_v, fin_o)
    rows, width = wq.shape
    quarter = width // 4
    span_levels = levels // 4
    own = clips * fr * sites
    pair = fr * sites
    total = 4 * own
    channels = embed_in.shape[0]
    heads = quarter // HEAD_DIM

    dp, wide = lax.axis_index("dp"), lax.axis_index("wide")
    p, c, z, s = dp // 2, dp % 2, wide // 2, wide % 2
    j = 2 * s + p

    def dev(p_, c_, z_, s_):
        return (p_ * 2 + c_, z_ * 2 + s_)

    sib, acr, mix = dev(p, 1 - c, z, s), dev(1 - p, c, z, s), dev(1 - p, 1 - c, z, s)
    bes, diag = dev(p, c, z, 1 - s), dev(1 - p, c, z, 1 - s)
    above, below = dev(p, c, z + 1, s), dev(p, c, z - 1, s)
    low, high = z > 0, z < levels - 1
    first, last = wide == 0, wide == n_wide - 1
    primary, other = c == s, c != s
    jz, lz = z // span_levels, z % span_levels
    peers = (None, sib, acr, mix)

    pend = []

    def go(cond, copy):
        guarded(cond, copy.start)
        pend.append((cond, copy))

    def arrive(cond, view, sem):
        guarded(cond, remote(view, view, sem, sem, sib).wait_recv)

    barrier = pltpu.get_barrier_semaphore()

    def greet(peer):
        pl.semaphore_signal(barrier, inc=1, device_id=peer, device_id_type=MESH)

    for peer in (sib, acr, mix, bes, diag):
        greet(peer)
    pl.when(high)(lambda: greet(above))
    pl.when(low)(lambda: greet(below))
    far_next, far_prev = both(s == 1, high), both(s == 0, low)
    pl.when(far_next)(lambda: greet((dp, wide + 1)))
    pl.when(far_prev)(lambda: greet((dp, wide - 1)))
    count = 5 + jnp.where(high, 1, 0) + jnp.where(low, 1, 0)
    count = count + jnp.where(s == 1, jnp.where(high, 1, 0), jnp.where(low, 1, 0))

    def shard(level, side):
        return span((level * 2 + side) * rows, rows)

    def quart(k):
        return span(k * quarter, quarter)

    locals_ = [
        pltpu.make_async_copy(frames, fbuf.at[:, pl.ds(fr, fr)], loc.at[0]),
        pltpu.make_async_copy(conv_in, conv, loc.at[1]),
        pltpu.make_async_copy(embed_in, embed, loc.at[2]),
    ]
    locals_ += [
        pltpu.make_async_copy(in_w[m].at[:, quart(j)], weights.at[m, shard(z, s)], loc.at[3 + m]) for m in range(3)
    ]
    own_og = [pltpu.make_async_copy(og_in.at[g * 2 + c], og.at[0, g], loc.at[6 + g]) for g in range(2)]
    own_o = pltpu.make_async_copy(wo, out_w.at[shard(lz, s)], loc.at[8])
    at_source = j == jz
    for copy in locals_ + own_og:
        copy.start()
    pl.when(at_source)(own_o.start)

    @pl.when(first)
    def _():
        fbuf[:, 0:fr] = jnp.zeros((clips, fr, sites, channels), BF16)

    pl.semaphore_wait(barrier, count)

    go(
        jnp.logical_not(last),
        remote(frames, fbuf.at[:, pl.ds(0, fr)], halo.at[0], halo.at[1], (dp, wide + 1)),
    )
    j_bes = 2 * (1 - s) + p
    for m in range(3):
        go(primary, remote(in_w[m].at[:, quart(j_bes)], weights.at[m, shard(z, s)], xw.at[0, m], xw.at[1, m], bes))

    def z_start(m):
        locals_[3 + m].wait()
        view = weights.at[m, shard(z, c)]
        arrive(other, view, xw.at[1, m])
        go(high, remote(view, view, zs.at[m, z, 0], zr.at[m, z], above))
        go(low, remote(view, view, zs.at[m, z, 1], zr.at[m, z], below))
        go(other, remote(view, view, bs.at[m, z], br.at[m, z], sib))

    def z_step(m, t):
        for down in range(2):
            valid = z + t <= levels - 1 if down else z >= t
            i = jnp.where(valid, z + t if down else z - t, z)
            view = weights.at[m, shard(i, c)]
            arrive(valid, view, zr.at[m, i])
            if t < levels - 1:
                peer = below if down else above
                go(both(valid, low if down else high), remote(view, view, zs.at[m, i, down], zr.at[m, i], peer))
            go(valid, remote(view, view, bs.at[m, i], br.at[m, i], sib))

    def z_done(m):
        for i in range(levels):
            arrive(jnp.logical_or(z != i, primary), weights.at[m, shard(i, 1 - c)], br.at[m, i])

    def o_view(i, side):
        return out_w.at[shard(i // 4, side), span((i % 4) * quarter, quarter)]

    def o_step(i):
        source = j * span_levels + i // 4
        view = o_view(i, c)
        here, up, down = z == source, z > source, z < source
        arrive(z != source, view, zr.at[3, i])
        go(both(z >= source, high), remote(view, view, zs.at[3, i, 0], zr.at[3, i], above))
        go(both(z <= source, low), remote(view, view, zs.at[3, i, 1], zr.at[3, i], below))
        go(jnp.logical_or(z != source, other), remote(view, view, bs.at[3, i], br.at[3, i], sib))

    def o_done():
        for i in range(levels):
            source = j * span_levels + i // 4
            arrive(jnp.logical_or(z != source, primary), o_view(i, 1 - c), br.at[3, i])

    def encode():
        arrive(jnp.logical_not(first), fbuf.at[:, pl.ds(0, fr)], halo.at[1])
        locals_[0].wait()
        locals_[1].wait()
        for clip in range(clips):
            raw = fbuf[clip].astype(F32)
            active = (raw / (1.0 + jnp.exp(-raw))).astype(BF16)
            acc = raw[fr:].reshape(pair, channels)
            for tap in range(3):
                moved = active[fr - tap : 2 * fr - tap].reshape(pair, channels)
                acc = acc + jnp.dot(moved, conv[tap], preferred_element_type=F32)
            enc[j, pl.ds(clip * pair, pair)] = acc.astype(BF16)
        for k, peer in enumerate((acr, bes, diag)):
            go(None, remote(enc.at[j], enc.at[j], es.at[k], er.at[k], peer))

    def embed_block(k):
        p_ = 1 - p if k in (1, 3) else p
        s_ = 1 - s if k in (2, 3) else s
        jb = 2 * s_ + p_
        if k:
            arrive(None, enc.at[jb], er.at[k - 1])
        else:
            locals_[2].wait()

        @pl.loop(0, own // pair)
        def _(i):
            at = span(i * pair, pair)
            token = jnp.dot(enc[jb, at], embed[...], preferred_element_type=F32).astype(BF16)
            if k < 2:
                tokens[span(p_ * own + i * pair, pair)] = token
            floats = token.astype(F32)
            center = floats - jnp.mean(floats, axis=-1, keepdims=True)
            spread = jnp.mean(center * center, axis=-1, keepdims=True)
            norm = (center * lax.rsqrt(spread + EPS)).astype(BF16)
            where = span(jb * own + i * pair, pair)
            normed[where] = norm
            normed_t[:, where] = norm.T

    def lane(ab, g, clip, f):
        return pick[:, pl.ds(((ab * 2 + g) * clips + clip) * fr + f, 1)]

    def og_send(g, f):
        for ab in range(1, 4):
            target = g * 2 + (1 - c if ab % 2 else c)
            go(None, remote(og_in.at[target, f], og.at[ab, g, f], gs.at[ab, g, f], gr.at[ab, g, f], peers[ab]))

    def slab_rows(side, g, clip, f, size):
        return span((((side * 2 + g) * clips + clip) * fr + f) * sites, size)

    def select(g, f):
        for ab in range(1, 4):
            arrive(None, og.at[ab, g, f], gr.at[ab, g, f])
        if f == 0:
            own_og[g].wait()
        for clip in range(clips):
            at = slab_rows(s, g, clip, f, sites)

            @pl.loop(0, 4)
            def _(k):
                cols = span(k * quarter, quarter)
                value = sum(og[ab, g, f, :, cols].astype(F32) * lane(ab, g, clip, f) for ab in range(4))
                upst[at, cols] = value.astype(BF16)

            view = upst.at[at]
            go(None, remote(view, view, us.at[g, f, clip], ur.at[g, f, clip], bes))

    def up_done():
        for g in range(2):
            for f in range(fr):
                for clip in range(clips):
                    arrive(None, upst.at[slab_rows(1 - s, g, clip, f, sites)], ur.at[g, f, clip])

    def project(m):
        z_done(m)

        @pl.loop(0, 4)
        def _(i):
            at = span(i * own, own)
            qkv[m, at] = jnp.dot(normed[at], weights[m], preferred_element_type=F32).astype(BF16)

    def wide_dot(x, y):
        return lax.dot_general(x, y, (((1,), (1,)), ((), ())), preferred_element_type=F32)

    def tall_dot(x, y):
        return lax.dot_general(x, y, (((0,), (0,)), ((), ())), preferred_element_type=F32)

    def attend():
        @pl.loop(0, total // pair)
        def _(b):
            at = span(b * pair, pair)
            frame_of = lax.broadcasted_iota(jnp.int32, (pair, pair), 0) // sites
            key_of = lax.broadcasted_iota(jnp.int32, (pair, pair), 1) // sites
            valid = jnp.logical_and(frame_of == key_of, klim[pl.ds(b % (2 * clips), 1), :] > 0)
            for h in range(heads):
                lanes = pl.ds(h * HEAD_DIM, HEAD_DIM)
                scores = jnp.where(valid, wide_dot(qkv[0, at, lanes], qkv[1, at, lanes]) * scale, masked_score)
                top = jnp.exp(scores - jnp.max(scores, axis=-1, keepdims=True))
                prob = top / jnp.sum(top, axis=-1, keepdims=True)
                probs[b, h] = prob
                att[at, lanes] = jnp.dot(
                    prob.astype(BF16), qkv[2, at, lanes], preferred_element_type=F32
                ).astype(BF16)
            att_t[:, at] = att[at, :].T

    def attend_back():
        @pl.loop(0, total // pair)
        def _(b):
            at = span(b * pair, pair)
            for h in range(heads):
                lanes = pl.ds(h * HEAD_DIM, HEAD_DIM)
                q, k, v, g = qkv[0, at, lanes], qkv[1, at, lanes], qkv[2, at, lanes], datt[at, lanes]
                prob = probs[b, h]
                d_probs = wide_dot(g, v)
                inner = jnp.sum(prob * d_probs, axis=-1, keepdims=True)
                d_scores = (prob * (d_probs - inner) * scale).astype(BF16)
                dqkv[0, at, lanes] = jnp.dot(d_scores, k, preferred_element_type=F32).astype(BF16)
                dqkv[1, at, lanes] = tall_dot(d_scores, q).astype(BF16)
                dqkv[2, at, lanes] = tall_dot(prob.astype(BF16), g).astype(BF16)

    def back_project():
        @pl.loop(0, 4)
        def _(i):
            at = span(i * own, own)
            datt[at] = wide_dot(upst[at], out_w[...]).astype(BF16)

    def partial_out(g):
        for clip in range(clips):
            at = slab_rows(1 - s, g, clip, 0, pair)
            to = pl.ds((g * clips + clip) * pair, pair)

            @pl.loop(0, 4)
            def _(k):
                cols = span(k * quarter, quarter)
                px_out[to, cols] = jnp.dot(att[at, :], out_w[:, cols], preferred_element_type=F32).astype(BF16)

            go(None, remote(px_out.at[to], px_in.at[to], ps.at[g, clip], pr.at[g, clip], bes))

    def combine(g):
        keep_tokens = jnp.where(p == 0, 1.0, 0.0).astype(F32)
        for clip in range(clips):
            at = slab_rows(s, g, clip, 0, pair)
            to = pl.ds((g * clips + clip) * pair, pair)
            arrive(None, px_in.at[to], pr.at[g, clip])

            @pl.loop(0, 4)
            def _(k):
                cols = span(k * quarter, quarter)
                value = jnp.dot(att[at, :], out_w[:, cols], preferred_element_type=F32)
                value = value + px_in[to, cols].astype(F32) + tokens[to, cols].astype(F32) * keep_tokens
                px_in[to, cols] = value.astype(BF16)

        for f in range(fr):
            for ab in (3, 2, 1, 0):
                slot = og.at[ab, g, f] if ab else y_in.at[0, g, f]

                @pl.loop(0, 4)
                def _(k):
                    cols = span(k * quarter, quarter)
                    value = sum(
                        px_in[pl.ds(((g * clips + clip) * fr + f) * sites, sites), cols].astype(F32)
                        * lane(ab, g, clip, f)
                        for clip in range(clips)
                    )
                    slot[:, cols] = value.astype(BF16)

                if ab:
                    go(None, remote(slot, y_in.at[ab, g, f], ys.at[ab, g, f], yr.at[ab, g, f], peers[ab]))

    def finish_out(g):
        for f in range(fr):
            for ab in range(1, 4):
                arrive(None, y_in.at[ab, g, f], yr.at[ab, g, f])
            for b in range(2):
                target = g * 2 + (1 - c if b else c)
                block_out[target, f] = (y_in[b, g, f].astype(F32) + y_in[2 + b, g, f].astype(F32)).astype(BF16)

    def term(m, i, side):
        if m < 3:
            return jnp.dot(normed_t[shard(i, side), :], dqkv[m], preferred_element_type=F32)
        return jnp.dot(
            att_t[shard(i // 4, side), :], upst[:, span((i % 4) * quarter, quarter)], preferred_element_type=F32
        )

    def emit(m):
        @pl.loop(0, levels)
        def _(i):
            term_out[m, i] = term(m, i, 1 - c).astype(BF16)

        go(None, remote(term_out.at[m], term_in.at[m], cs.at[m], cr.at[m], sib))

    def fold(m):
        arrive(None, term_in.at[m], cr.at[m])

        @pl.loop(0, levels)
        def _(i):
            keep[m, i] = (term(m, i, c) + term_in[m, i].astype(F32)).astype(BF16)

    def target(m, i):
        return i if m < 3 else j * span_levels + i // 4

    def add_in(m, i, source, sem):
        arrive(None, source.at[m, i], sem.at[m, i])
        keep[m, i] = (keep[m, i].astype(F32) + source[m, i].astype(F32)).astype(BF16)

    def pass_on(m):
        for k in range(levels):
            i = jnp.where(z < levels // 2, levels - 1 - k, k) if m < 3 else k
            d = target(m, i)
            upward, downward = z < d, z > d
            pl.when(both(upward, low))(lambda: add_in(m, i, from_low, rl))
            pl.when(both(downward, high))(lambda: add_in(m, i, from_high, rh))
            view = keep.at[m, i]
            go(upward, remote(view, from_low.at[m, i], rs.at[m, i], rl.at[m, i], above))
            go(downward, remote(view, from_high.at[m, i], rs.at[m, i], rh.at[m, i], below))

    def settle(m):
        fin = fins[m]
        if m < 3:
            pl.when(low)(lambda: add_in(m, z, from_low, rl))
            pl.when(high)(lambda: add_in(m, z, from_high, rh))
            view, place = keep.at[m, z], fin.at[:, quart(j)]
            go(other, remote(view, place, a_s.at[m, 0], a_r.at[m, 0], bes))

            @pl.when(primary)
            def _():
                fin[:, quart(j)] = keep[m, z]

            go(primary, remote(view, place, b_s.at[m, 0], b_r.at[m, 0], acr))
        else:
            for piece in range(4):
                i = lz * 4 + piece
                cols = pl.ds(piece * quarter, quarter)
                pl.when(both(at_source, low))(lambda: add_in(m, i, from_low, rl))
                pl.when(both(at_source, high))(lambda: add_in(m, i, from_high, rh))
                go(
                    both(at_source, other),
                    remote(keep.at[m, i], fin.at[:, cols], a_s.at[m, piece], a_r.at[m, piece], bes),
                )

                @pl.when(both(at_source, primary))
                def _():
                    fin[:, cols] = keep[m, i]

    def spread(m):
        fin = fins[m]
        if m < 3:
            place = fin.at[:, quart(j_bes)]
            arrive(primary, place, a_r.at[m, 0])
            go(primary, remote(place, place, b_s.at[m, 1], b_r.at[m, 1], acr))
        else:
            p_z = jz % 2
            for piece in range(4):
                arrive(both(primary, j_bes == jz), fin.at[:, pl.ds(piece * quarter, quarter)], a_r.at[m, piece])
            go(both(primary, p == p_z), remote(fin, fin, b_s.at[m, 0], b_r.at[m, 0], acr))

    def share(m):
        fin = fins[m]
        if m < 3:
            for k, side in enumerate((s, 1 - s)):
                arrive(primary, fin.at[:, quart(2 * side + 1 - p)], b_r.at[m, k])
        else:
            arrive(both(primary, p != jz % 2), fin, b_r.at[m, 0])
        go(primary, remote(fin, fin, f_s.at[m], f_r.at[m], sib))

    def complete(m):
        arrive(other, fins[m], f_r.at[m])

    pieces = [(g, f) for g in range(2) for f in range(fr)]
    z_start(0)
    encode()
    z_start(1)
    z_start(2)
    for piece in pieces:
        og_send(*piece)
    go(
        both(primary, j_bes == jz),
        remote(wo, out_w.at[shard(lz, s)], xo.at[0], xo.at[1], bes),
    )
    steps = sorted((m + t - 1, t, m) for m in range(3) for t in range(1, levels))
    embed_block(0)
    cuts = [len(steps) * k // 6 for k in range(4)]
    for k in range(3):
        for _, t, m in steps[cuts[k] : cuts[k + 1]]:
            z_step(m, t)
        embed_block(k + 1)
    pl.when(at_source)(own_o.wait)
    arrive(both(at_source, other), out_w.at[shard(lz, c)], xo.at[1])
    for _, t, m in steps[cuts[3] :]:
        z_step(m, t)
    select(*pieces[0])
    o_step(0)
    project(0)
    o_step(1)
    project(1)
    for i in range(2, levels):
        o_step(i)
    select(*pieces[1])
    project(2)
    attend()
    for piece in pieces[2:]:
        select(*piece)
    o_done()
    partial_out(0)
    partial_out(1)
    up_done()
    back_project()
    emit(3)
    attend_back()
    fold(3)
    emit(2)
    pass_on(3)
    fold(2)
    emit(1)
    pass_on(2)
    fold(1)
    emit(0)
    settle(3)
    combine(0)
    pass_on(1)
    fold(0)
    settle(2)
    spread(3)
    pass_on(0)
    combine(1)
    settle(1)
    spread(2)
    share(3)
    settle(0)
    spread(1)
    share(2)
    finish_out(0)
    spread(0)
    share(1)
    finish_out(1)
    share(0)
    for m in (3, 2, 1, 0):
        complete(m)
    for cond, copy in pend:
        guarded(cond, copy.wait_send)


def run_block(n_wide, frames, conv_w, embed_w, wq, wk, wv, wo, out_grad, pick, klim):
    clips, fr, sites, channels = frames.shape
    rows, width = wq.shape
    quarter, levels = width // 4, n_wide // 2
    own, pair = clips * fr * sites, fr * sites
    total = 4 * own
    heads = quarter // HEAD_DIM
    dma = pltpu.SemaphoreType.DMA
    anywhere = pl.BlockSpec(memory_space=pl.ANY)
    vmem = pl.BlockSpec(memory_space=pltpu.VMEM)

    def buf(*shape, dtype=BF16):
        return pltpu.VMEM(shape, dtype)

    scratch = [
        buf(clips, 2 * fr, sites, channels),
        buf(3, channels, channels),
        buf(channels, width),
        buf(3, width, quarter),
        buf(quarter, width),
        buf(4, own, channels),
        buf(2 * own, width),
        buf(total, width),
        buf(width, total),
        buf(4, 2, fr, sites, width),
        buf(total, width),
        buf(3, total, quarter),
        buf(total, quarter),
        buf(total, quarter),
        buf(quarter, total),
        buf(3, total, quarter),
        buf(total // pair, heads, pair, pair, dtype=F32),
        buf(2 * own, width),
        buf(2 * own, width),
        buf(4, 2, fr, sites, width),
        *([buf(4, levels, rows, quarter)] * 5),
        dma((9,)),
        dma((2,)),
        dma((2, 3)),
        dma((2,)),
        dma((4, levels, 2)),
        dma((4, levels)),
        dma((4, levels)),
        dma((4, levels)),
        dma((3,)),
        dma((3,)),
        dma((4, 2, fr)),
        dma((4, 2, fr)),
        dma((2, fr, clips)),
        dma((2, fr, clips)),
        dma((2, clips)),
        dma((2, clips)),
        dma((4, 2, fr)),
        dma((4, 2, fr)),
        dma((4,)),
        dma((4,)),
        dma((4, levels)),
        dma((4, levels)),
        dma((4, levels)),
        dma((4, 4)),
        dma((4, 4)),
        dma((4, 2)),
        dma((4, 2)),
        dma((4,)),
        dma((4,)),
    ]
    return pl.pallas_call(
        functools.partial(kernel, n_wide, clips, fr, sites, 1.0 / math.sqrt(HEAD_DIM)),
        out_shape=[jax.ShapeDtypeStruct(out_grad.shape, BF16)]
        + [jax.ShapeDtypeStruct((rows, width), BF16)] * 4,
        in_specs=[anywhere] * 8 + [vmem] * 2,
        out_specs=[vmem] * 5,
        scratch_shapes=scratch,
        compiler_params=pltpu.CompilerParams(
            collective_id=0, has_side_effects=True, vmem_limit_bytes=63 * 1024 * 1024
        ),
        cost_estimate=pl.CostEstimate(flops=12_000_000_000, bytes_accessed=20_000_000, transcendentals=0),
        name="section",
    )(frames, conv_w, embed_w, wq, wk, wv, wo, out_grad, pick, klim)


def body(
    frames,
    conv_weight,
    embed_weight,
    query_weight,
    key_weight,
    value_weight,
    output_weight,
    out_grad,
    bucket_owner,
    clip_bucket,
    clip_frames,
    clip_grid,
):
    n_wide = lax.axis_size("wide")
    dp, slab = lax.axis_index("dp"), lax.axis_index("wide")
    p, c = dp // 2, dp % 2
    clips, fr, sites = frames.shape[1:4]
    buckets = bucket_owner.shape[0]
    table = (clip_bucket[:, :, None] == jnp.arange(buckets, dtype=jnp.int32)).astype(jnp.int32)
    owners = jnp.sum(table * bucket_owner, axis=-1)
    grid_tokens = clip_grid[..., 0] * clip_grid[..., 1]

    def own_parity(values):
        values = values.reshape(2, 2, clips)
        return jnp.where(c == 0, values[:, 0], values[:, 1])

    owner, live_frames, live_tokens = own_parity(owners), own_parity(clip_frames), own_parity(grid_tokens)
    key_tokens = jnp.where(live_tokens > 0, live_tokens, sites)
    site = jnp.arange(sites, dtype=jnp.int32)
    klim = (site[None, None, None, :] < key_tokens[:, :, None, None]) & jnp.ones((2, clips, fr, sites), bool)
    klim = klim.reshape(2 * clips, fr * sites).astype(F32)
    ab = jnp.arange(4, dtype=jnp.int32)
    to = ((ab // 2) ^ p) * 2 + ((ab % 2) ^ c)
    frame = slab * fr + jnp.arange(fr, dtype=jnp.int32)
    hit = to[:, None, None] == owner
    live = frame < live_frames[:, :, None]
    lanes = (hit[..., None] & live[None]).reshape(-1)
    limit = jnp.broadcast_to(live_tokens[None, :, :, None], (4, 2, clips, fr)).reshape(-1)
    pick = (lanes[None, :] & (site[:, None] < limit[None, :])).astype(F32)
    block, grad_q, grad_k, grad_v, grad_o = run_block(
        n_wide,
        frames[0],
        conv_weight,
        embed_weight,
        query_weight,
        key_weight,
        value_weight,
        output_weight,
        out_grad[0],
        pick,
        klim,
    )
    return (block[None], *(g.astype(F32) for g in (grad_q, grad_k, grad_v, grad_o)))


def solution(mesh):
    rows = P("wide", None)
    slabs = P("dp", None, "wide", None, None)
    in_specs = (slabs, P(), P(), rows, rows, rows, rows, slabs, P(), P(), P(), P())
    out_specs = (slabs, rows, rows, rows, rows)
    return jax.shard_map(body, mesh=mesh, in_specs=in_specs, out_specs=out_specs, check_vma=False)
```

```python
import functools
import math

import jax
import jax.numpy as jnp
from jax import lax
from jax.experimental import pallas as pl
from jax.experimental.pallas import tpu as pltpu
from jax.sharding import PartitionSpec as P

HEAD_DIM = 128
MESH = pl.DeviceIdType.MESH
EPS = 1e-06
masked_score = -1e30
F32, BF16 = jnp.float32, jnp.bfloat16


def remote(src, dst, send, recv, peer):
    return pltpu.make_async_remote_copy(
        src_ref=src, dst_ref=dst, send_sem=send, recv_sem=recv, device_id=peer, device_id_type=MESH
    )


def span(start, size):
    return pl.ds(pl.multiple_of(start, 128 if size % 128 == 0 else 16), size)


def both(*conds):
    out = None
    for cond in conds:
        if cond is not None:
            out = cond if out is None else jnp.logical_and(out, cond)
    return out


def guarded(cond, action):
    if cond is None:
        action()
    else:
        pl.when(cond)(action)


def kernel(n_wide, clips, fr, sites, scale, *refs):
    frames, conv_in, embed_in, wq, wk, wv, wo, og_in, pick, klim = refs[:10]
    block_out, fin_q, fin_k, fin_v, fin_o = refs[10:15]
    (
        fbuf, conv, embed, weights, out_w, enc, tokens, normed, normed_t, og, upst, qkv, datt, datt_x, att, att_x,
        att_t, dqkv, probs, comb, y_in, term_out, term_in, keep, keep_x, from_low, from_high,
    ) = refs[15:42]
    (
        loc, halo, xw, xo, zs, zr, bs, br, os_, or_, ds, dr, es, er, gs, gr, us, ur, ps, pr, ys, yr, cs, cr, ks,
        rs, rl, rh, a_s, a_r, b_s, b_r, f_s, f_r,
    ) = refs[42:]
    levels = n_wide // 2
    in_w = (wq, wk, wv)
    fins = (fin_q, fin_k, fin_v, fin_o)
    rows, width = wq.shape
    quarter = width // 4
    span_levels = levels // 4
    own = clips * fr * sites
    pair = fr * sites
    total = 4 * own
    channels = embed_in.shape[0]
    heads = quarter // HEAD_DIM

    dp, wide = lax.axis_index("dp"), lax.axis_index("wide")
    p, c, z, s = dp // 2, dp % 2, wide // 2, wide % 2
    j = 2 * s + p

    def dev(p_, c_, z_, s_):
        return (p_ * 2 + c_, z_ * 2 + s_)

    sib, acr, mix = dev(p, 1 - c, z, s), dev(1 - p, c, z, s), dev(1 - p, 1 - c, z, s)
    bes, diag = dev(p, c, z, 1 - s), dev(1 - p, c, z, 1 - s)
    above, below = dev(p, c, z + 1, s), dev(p, c, z - 1, s)
    low, high = z > 0, z < levels - 1
    first, last = wide == 0, wide == n_wide - 1
    primary, other = c == s, c != s
    jz, lz = z // span_levels, z % span_levels
    peers = (None, sib, acr, mix)

    pend = []

    def go(cond, copy):
        guarded(cond, copy.start)
        pend.append((cond, copy))

    def arrive(cond, view, sem):
        guarded(cond, remote(view, view, sem, sem, sib).wait_recv)

    barrier = pltpu.get_barrier_semaphore()

    def greet(peer):
        pl.semaphore_signal(barrier, inc=1, device_id=peer, device_id_type=MESH)

    for peer in (sib, acr, mix, bes, diag):
        greet(peer)
    pl.when(high)(lambda: greet(above))
    pl.when(low)(lambda: greet(below))
    far_next, far_prev = both(s == 1, high), both(s == 0, low)
    pl.when(far_next)(lambda: greet((dp, wide + 1)))
    pl.when(far_prev)(lambda: greet((dp, wide - 1)))
    count = 5 + jnp.where(high, 1, 0) + jnp.where(low, 1, 0)
    count = count + jnp.where(s == 1, jnp.where(high, 1, 0), jnp.where(low, 1, 0))

    def shard(level, side):
        return span((level * 2 + side) * rows, rows)

    def quart(k):
        return span(k * quarter, quarter)

    locals_ = [
        pltpu.make_async_copy(frames, fbuf.at[:, pl.ds(fr, fr)], loc.at[0]),
        pltpu.make_async_copy(conv_in, conv, loc.at[1]),
        pltpu.make_async_copy(embed_in, embed, loc.at[2]),
    ]
    locals_ += [
        pltpu.make_async_copy(in_w[m].at[:, quart(j)], weights.at[m, shard(z, s)], loc.at[3 + m]) for m in range(3)
    ]
    own_og = [pltpu.make_async_copy(og_in.at[g * 2 + c], og.at[0, g], loc.at[6 + g]) for g in range(2)]
    own_o = pltpu.make_async_copy(wo, out_w.at[0, shard(lz, s)], loc.at[8])
    at_source = j == jz
    for copy in locals_ + own_og:
        copy.start()
    pl.when(at_source)(own_o.start)

    @pl.when(first)
    def _():
        fbuf[:, 0:fr] = jnp.zeros((clips, fr, sites, channels), BF16)

    pl.semaphore_wait(barrier, count)

    go(
        jnp.logical_not(last),
        remote(frames, fbuf.at[:, pl.ds(0, fr)], halo.at[0], halo.at[1], (dp, wide + 1)),
    )
    j_bes = 2 * (1 - s) + p
    for m in range(3):
        go(primary, remote(in_w[m].at[:, quart(j_bes)], weights.at[m, shard(z, s)], xw.at[0, m], xw.at[1, m], bes))

    def z_start(m):
        locals_[3 + m].wait()
        view = weights.at[m, shard(z, c)]
        arrive(other, view, xw.at[1, m])
        go(high, remote(view, view, zs.at[m, z, 0], zr.at[m, z], above))
        go(low, remote(view, view, zs.at[m, z, 1], zr.at[m, z], below))
        go(other, remote(view, view, bs.at[m, z], br.at[m, z], sib))

    def z_step(m, t):
        for down in range(2):
            valid = z + t <= levels - 1 if down else z >= t
            i = jnp.where(valid, z + t if down else z - t, z)
            view = weights.at[m, shard(i, c)]
            arrive(valid, view, zr.at[m, i])
            if t < levels - 1:
                peer = below if down else above
                go(both(valid, low if down else high), remote(view, view, zs.at[m, i, down], zr.at[m, i], peer))
            go(valid, remote(view, view, bs.at[m, i], br.at[m, i], sib))

    def z_done(m):
        for i in range(levels):
            arrive(jnp.logical_or(z != i, primary), weights.at[m, shard(i, 1 - c)], br.at[m, i])

    def o_view(q, i, side):
        return out_w.at[q, shard(i // 4, side), span((i % 4) * quarter, quarter)]

    def o_start():
        pl.when(at_source)(own_o.wait)
        arrive(both(at_source, other), out_w.at[0, shard(lz, c)], xo.at[1])

    def o_step(i):
        source = j * span_levels + i // 4
        view = o_view(0, i, c)
        arrive(z != source, view, zr.at[3, i])
        go(both(z >= source, high), remote(view, view, zs.at[3, i, 0], zr.at[3, i], above))
        go(both(z <= source, low), remote(view, view, zs.at[3, i, 1], zr.at[3, i], below))
        go(None, remote(view, o_view(1, i, c), os_.at[i], or_.at[i], bes))
        go(jnp.logical_or(z != source, other), remote(view, view, bs.at[3, i], br.at[3, i], sib))

    def o_cross(i):
        view = o_view(1, i, c)
        arrive(None, view, or_.at[i])
        go(None, remote(view, view, ds.at[i], dr.at[i], sib))

    def o_done():
        for i in range(levels):
            source = j * span_levels + i // 4
            arrive(jnp.logical_or(z != source, primary), o_view(0, i, 1 - c), br.at[3, i])
            arrive(None, o_view(1, i, 1 - c), dr.at[i])

    def encode():
        arrive(jnp.logical_not(first), fbuf.at[:, pl.ds(0, fr)], halo.at[1])
        locals_[0].wait()
        locals_[1].wait()
        for clip in range(clips):
            raw = fbuf[clip].astype(F32)
            active = (raw / (1.0 + jnp.exp(-raw))).astype(BF16)
            acc = raw[fr:].reshape(pair, channels)
            for tap in range(3):
                moved = active[fr - tap : 2 * fr - tap].reshape(pair, channels)
                acc = acc + jnp.dot(moved, conv[tap], preferred_element_type=F32)
            enc[j, pl.ds(clip * pair, pair)] = acc.astype(BF16)
        for k, peer in enumerate((acr, bes, diag)):
            go(None, remote(enc.at[j], enc.at[j], es.at[k], er.at[k], peer))

    def embed_block(k):
        p_ = 1 - p if k in (1, 3) else p
        s_ = 1 - s if k in (2, 3) else s
        jb = 2 * s_ + p_
        if k:
            arrive(None, enc.at[jb], er.at[k - 1])
        else:
            locals_[2].wait()

        @pl.loop(0, own // pair)
        def _(i):
            at = span(i * pair, pair)
            token = jnp.dot(enc[jb, at], embed[...], preferred_element_type=F32).astype(BF16)
            if k < 2:
                tokens[span(p_ * own + i * pair, pair)] = token
            floats = token.astype(F32)
            center = floats - jnp.mean(floats, axis=-1, keepdims=True)
            spread = jnp.mean(center * center, axis=-1, keepdims=True)
            norm = (center * lax.rsqrt(spread + EPS)).astype(BF16)
            where = span(jb * own + i * pair, pair)
            normed[where] = norm
            turned = norm.T
            for k_ in range(n_wide):
                normed_t[k_ % 2, pl.ds(k_ // 2 * rows, rows), where] = turned[k_ * rows : (k_ + 1) * rows]

    def lane(ab, g, clip, f):
        return pick[:, pl.ds(((ab * 2 + g) * clips + clip) * fr + f, 1)]

    def og_send(g, f):
        for ab in range(1, 4):
            target = g * 2 + (1 - c if ab % 2 else c)
            go(None, remote(og_in.at[target, f], og.at[ab, g, f], gs.at[ab, g, f], gr.at[ab, g, f], peers[ab]))

    def slab_rows(side, g, size):
        return span((side * 2 + g) * own, size)

    def select(g, f):
        for ab in range(1, 4):
            arrive(None, og.at[ab, g, f], gr.at[ab, g, f])
        if f == 0:
            own_og[g].wait()
        for clip in range(clips):
            at = pl.ds(((g * clips + clip) * fr + f) * sites, sites)

            @pl.loop(0, 4)
            def _(k):
                cols = span(k * quarter, quarter)
                value = sum(og[ab, g, f, :, cols] * lane(ab, g, clip, f) for ab in range(4))
                upst[at, cols] = value

    def project(m):
        z_done(m)

        @pl.loop(0, 2)
        def _(i):
            at = span(i * 2 * own, 2 * own)
            qkv[m, at] = jnp.dot(normed[at], weights[m], preferred_element_type=F32).astype(BF16)

    def wide_dot(x, y):
        return lax.dot_general(x, y, (((1,), (1,)), ((), ())), preferred_element_type=F32)

    def tall_dot(x, y):
        return lax.dot_general(x, y, (((0,), (0,)), ((), ())), preferred_element_type=F32)

    def attend(side):
        @pl.loop(0, 2 * clips)
        def _(k):
            b = side * 2 * clips + k
            at = span(b * pair, pair)
            frame_of = lax.broadcasted_iota(jnp.int32, (pair, pair), 0) // sites
            key_of = lax.broadcasted_iota(jnp.int32, (pair, pair), 1) // sites
            valid = jnp.logical_and(frame_of == key_of, klim[pl.ds(k, 1), :] > 0)
            for h in range(heads):
                lanes = pl.ds(h * HEAD_DIM, HEAD_DIM)
                scores = jnp.where(valid, wide_dot(qkv[0, at, lanes], qkv[1, at, lanes]) * scale, masked_score)
                top = jnp.exp(scores - jnp.max(scores, axis=-1, keepdims=True))
                prob = top * (1.0 / jnp.sum(top, axis=-1, keepdims=True))
                probs[b, h] = prob
                att[at, lanes] = jnp.dot(
                    prob.astype(BF16), qkv[2, at, lanes], preferred_element_type=F32
                ).astype(BF16)

    def att_send():
        at = slab_rows(1 - s, 0, 2 * own)
        go(None, remote(att.at[at], att_x, ps.at[0], pr.at[0], bes))

    def turn(q):
        if q:
            arrive(None, att_x, pr.at[0])

        @pl.loop(0, 2 * own // pair)
        def _(i):
            to = span(i * pair, pair)
            block = att_x[to] if q else att[span(s * 2 * own + i * pair, pair)]
            turned = block.T
            for k_ in range(2 * span_levels):
                att_t[q, k_ % 2, pl.ds(k_ // 2 * rows, rows), to] = turned[k_ * rows : (k_ + 1) * rows]

    def attend_back(side):
        @pl.loop(0, 2 * clips)
        def _(k):
            b = side * 2 * clips + k
            at = span(b * pair, pair)
            for h in range(heads):
                lanes = pl.ds(h * HEAD_DIM, HEAD_DIM)
                q, k_, v, g = qkv[0, at, lanes], qkv[1, at, lanes], qkv[2, at, lanes], datt[at, lanes]
                prob = probs[b, h]
                d_probs = wide_dot(g, v)
                inner = jnp.sum(prob * d_probs, axis=-1, keepdims=True)
                d_scores = (prob * (d_probs - inner) * scale).astype(BF16)
                dqkv[0, at, lanes] = jnp.dot(d_scores, k_, preferred_element_type=F32).astype(BF16)
                dqkv[1, at, lanes] = tall_dot(d_scores, q).astype(BF16)
                dqkv[2, at, lanes] = tall_dot(prob.astype(BF16), g).astype(BF16)

    def back_project(q):
        for g in range(2):
            at = pl.ds(g * own, own)
            value = wide_dot(upst[at], out_w[q]).astype(BF16)
            if q:
                datt_x[at] = value
            else:
                datt[slab_rows(s, g, own)] = value
        if q:
            go(None, remote(datt_x, datt.at[slab_rows(s, 0, 2 * own)], us.at[0], ur.at[0], bes))

    def datt_done():
        arrive(None, datt.at[slab_rows(1 - s, 0, 2 * own)], ur.at[0])

    def combine(g):
        keep_tokens = jnp.where(p == 0, 1.0, 0.0).astype(F32)
        at, to = slab_rows(s, g, own), pl.ds(g * own, own)

        @pl.loop(0, 4)
        def _(k):
            cols = span(k * quarter, quarter)
            value = jnp.dot(att[at], out_w[0, :, cols], preferred_element_type=F32)
            value = value + jnp.dot(att_x[to], out_w[1, :, cols], preferred_element_type=F32)
            comb[to, cols] = (value + tokens[to, cols].astype(F32) * keep_tokens).astype(BF16)

        for f in range(fr):
            for ab in (3, 2, 1, 0):
                slot = og.at[ab, g, f] if ab else y_in.at[0, g, f]

                @pl.loop(0, 4)
                def _(k):
                    cols = span(k * quarter, quarter)
                    slot[:, cols] = sum(
                        comb[pl.ds(((g * clips + clip) * fr + f) * sites, sites), cols] * lane(ab, g, clip, f)
                        for clip in range(clips)
                    )

                if ab:
                    go(None, remote(slot, y_in.at[ab, g, f], ys.at[ab, g, f], yr.at[ab, g, f], peers[ab]))

    def finish_out(g):
        for f in range(fr):
            for ab in range(1, 4):
                arrive(None, y_in.at[ab, g, f], yr.at[ab, g, f])
            for b in range(2):
                target = g * 2 + (1 - c if b else c)
                block_out[target, f] = (y_in[b, g, f].astype(F32) + y_in[2 + b, g, f].astype(F32)).astype(BF16)

    def message(m, i):
        return span(i * rows, rows)

    def terms(m, side, put):
        if m < 3:

            @pl.loop(0, 2)
            def _(i):
                at = span(i * (width // 4), width // 4)
                put(at, jnp.dot(normed_t[side, at], dqkv[m], preferred_element_type=F32))
        else:

            @pl.loop(0, 4)
            def _(piece):
                cols = span(piece * quarter, quarter)
                value = jnp.dot(att_t[m - 3, side], upst[:, cols], preferred_element_type=F32)
                for k in range(span_levels):
                    put(span((k * 4 + piece) * rows, rows), value[k * rows : (k + 1) * rows])

    def emit(m):
        def put(at, value):
            term_out[m, at] = value.astype(BF16)

        terms(m, 1 - c, put)
        go(None, remote(term_out.at[m], term_in.at[m], cs.at[m], cr.at[m], sib))

    def fold(m):
        arrive(None, term_in.at[m], cr.at[m])
        if m == 3:
            arrive(None, keep_x, ks.at[1])

        def put(at, value):
            value = value + term_in[m, at].astype(F32)
            if m == 3:
                value = value + keep_x[at].astype(F32)
            keep[m, at] = value.astype(BF16)

        terms(m, c, put)
        if m == 4:
            go(None, remote(keep.at[4], keep_x, ks.at[0], ks.at[1], bes))

    def target(m, i):
        return i if m < 3 else j * span_levels + i // 4

    def add_in(m, i, source, sem):
        at = message(m, i)
        arrive(None, source.at[m, at], sem.at[m, i])
        keep[m, at] = (keep[m, at].astype(F32) + source[m, at].astype(F32)).astype(BF16)

    def pass_on(m):
        for k in range(levels):
            i = jnp.where(z < levels // 2, levels - 1 - k, k) if m < 3 else k
            d = target(m, i)
            upward, downward = z < d, z > d
            pl.when(both(upward, low))(lambda: add_in(m, i, from_low, rl))
            pl.when(both(downward, high))(lambda: add_in(m, i, from_high, rh))
            at = message(m, i)
            view = keep.at[m, at]
            go(upward, remote(view, from_low.at[m, at], rs.at[m, i], rl.at[m, i], above))
            go(downward, remote(view, from_high.at[m, at], rs.at[m, i], rh.at[m, i], below))

    def settle(m):
        fin = fins[m]
        if m < 3:
            pl.when(low)(lambda: add_in(m, z, from_low, rl))
            pl.when(high)(lambda: add_in(m, z, from_high, rh))
            view, place = keep.at[m, message(m, z)], fin.at[:, quart(j)]
            go(other, remote(view, place, a_s.at[m, 0], a_r.at[m, 0], bes))

            @pl.when(primary)
            def _():
                fin[:, quart(j)] = keep[m, message(m, z)]

            go(primary, remote(view, place, b_s.at[m, 0], b_r.at[m, 0], acr))
        else:
            for piece in range(4):
                i = lz * 4 + piece
                cols = pl.ds(piece * quarter, quarter)
                pl.when(both(at_source, low))(lambda: add_in(m, i, from_low, rl))
                pl.when(both(at_source, high))(lambda: add_in(m, i, from_high, rh))
                go(
                    both(at_source, other),
                    remote(keep.at[m, message(m, i)], fin.at[:, cols], a_s.at[m, piece], a_r.at[m, piece], bes),
                )

                @pl.when(both(at_source, primary))
                def _():
                    fin[:, cols] = keep[m, message(m, i)]

    def spread(m):
        fin = fins[m]
        if m < 3:
            place = fin.at[:, quart(j_bes)]
            arrive(primary, place, a_r.at[m, 0])
            go(primary, remote(place, place, b_s.at[m, 1], b_r.at[m, 1], acr))
        else:
            p_z = jz % 2
            for piece in range(4):
                arrive(both(primary, j_bes == jz), fin.at[:, pl.ds(piece * quarter, quarter)], a_r.at[m, piece])
            go(both(primary, p == p_z), remote(fin, fin, b_s.at[m, 0], b_r.at[m, 0], acr))

    def share(m):
        fin = fins[m]
        if m < 3:
            for k, side in enumerate((s, 1 - s)):
                arrive(primary, fin.at[:, quart(2 * side + 1 - p)], b_r.at[m, k])
        else:
            arrive(both(primary, p != jz % 2), fin, b_r.at[m, 0])
        go(primary, remote(fin, fin, f_s.at[m], f_r.at[m], sib))

    def complete(m):
        arrive(other, fins[m], f_r.at[m])

    pieces = [(g, f) for g in range(2) for f in range(fr)]
    steps = [(t, m) for t in range(1, levels) for m in range(3)]
    done = [0]

    def advance(k):
        while done[0] < len(steps) * k // 9:
            t, m = steps[done[0]]
            z_step(m, t)
            done[0] += 1

    z_start(0)
    og_send(*pieces[0])
    encode()
    z_start(1)
    z_start(2)
    for piece in pieces[1:]:
        og_send(*piece)
    go(
        both(primary, j_bes == jz),
        remote(wo, out_w.at[0, shard(lz, s)], xo.at[0], xo.at[1], bes),
    )
    for k in range(4):
        advance(k + 1)
        embed_block(k)
    advance(5)
    select(*pieces[0])
    advance(7)
    project(0)
    select(*pieces[1])
    advance(8)
    project(1)
    advance(9)
    project(2)
    o_start()
    o_step(0)
    attend(1 - s)
    att_send()
    o_step(1)
    select(*pieces[2])
    for i in range(2, levels - 1):
        o_step(i)
    o_cross(0)
    attend(s)
    turn(0)
    o_step(levels - 1)
    for piece in pieces[3:]:
        select(*piece)
    for i in range(1, levels):
        o_cross(i)
    o_done()
    back_project(1)
    turn(1)
    emit(4)
    combine(0)
    back_project(0)
    fold(4)
    emit(3)
    attend_back(s)
    datt_done()
    attend_back(1 - s)
    emit(2)
    fold(3)
    pass_on(3)
    fold(2)
    emit(1)
    pass_on(2)
    combine(1)
    fold(1)
    emit(0)
    settle(3)
    pass_on(1)
    fold(0)
    settle(2)
    spread(3)
    pass_on(0)
    settle(1)
    spread(2)
    share(3)
    finish_out(0)
    settle(0)
    spread(1)
    share(2)
    spread(0)
    share(1)
    finish_out(1)
    share(0)
    for m in (3, 2, 1, 0):
        complete(m)
    for cond, copy in pend:
        guarded(cond, copy.wait_send)


def run_block(n_wide, frames, conv_w, embed_w, wq, wk, wv, wo, out_grad, pick, klim):
    clips, fr, sites, channels = frames.shape
    rows, width = wq.shape
    quarter, levels = width // 4, n_wide // 2
    own, pair = clips * fr * sites, fr * sites
    total = 4 * own
    heads = quarter // HEAD_DIM
    dma = pltpu.SemaphoreType.DMA
    anywhere = pl.BlockSpec(memory_space=pl.ANY)
    vmem = pl.BlockSpec(memory_space=pltpu.VMEM)

    def buf(*shape, dtype=BF16):
        return pltpu.VMEM(shape, dtype)

    reach = levels * rows
    scratch = [
        buf(clips, 2 * fr, sites, channels),
        buf(3, channels, channels),
        buf(channels, width),
        buf(3, width, quarter),
        buf(2, quarter, width),
        buf(4, own, channels),
        buf(2 * own, width),
        buf(total, width),
        buf(2, width // 2, total),
        buf(4, 2, fr, sites, width),
        buf(2 * own, width),
        buf(3, total, quarter),
        buf(total, quarter),
        buf(2 * own, quarter),
        buf(total, quarter),
        buf(2 * own, quarter),
        buf(2, 2, quarter // 2, 2 * own),
        buf(3, total, quarter),
        buf(total // pair, heads, pair, pair, dtype=F32),
        buf(2 * own, width),
        buf(4, 2, fr, sites, width),
        buf(5, reach, quarter),
        buf(5, reach, quarter),
        buf(5, reach, quarter),
        buf(reach, quarter),
        buf(4, reach, quarter),
        buf(4, reach, quarter),
        dma((9,)),
        dma((2,)),
        dma((2, 3)),
        dma((2,)),
        dma((4, levels, 2)),
        dma((4, levels)),
        dma((4, levels)),
        dma((4, levels)),
        *([dma((levels,))] * 4),
        dma((3,)),
        dma((3,)),
        dma((4, 2, fr)),
        dma((4, 2, fr)),
        *([dma((1,))] * 4),
        dma((4, 2, fr)),
        dma((4, 2, fr)),
        dma((5,)),
        dma((5,)),
        dma((2,)),
        dma((4, levels)),
        dma((4, levels)),
        dma((4, levels)),
        dma((4, 4)),
        dma((4, 4)),
        dma((4, 2)),
        dma((4, 2)),
        dma((4,)),
        dma((4,)),
    ]
    return pl.pallas_call(
        functools.partial(kernel, n_wide, clips, fr, sites, 1.0 / math.sqrt(HEAD_DIM)),
        out_shape=[jax.ShapeDtypeStruct(out_grad.shape, BF16)]
        + [jax.ShapeDtypeStruct((rows, width), BF16)] * 4,
        in_specs=[anywhere] * 8 + [vmem] * 2,
        out_specs=[vmem] * 5,
        scratch_shapes=scratch,
        compiler_params=pltpu.CompilerParams(
            collective_id=0, has_side_effects=True, vmem_limit_bytes=63 * 1024 * 1024
        ),
        cost_estimate=pl.CostEstimate(flops=12_000_000_000, bytes_accessed=20_000_000, transcendentals=0),
        name="section",
    )(frames, conv_w, embed_w, wq, wk, wv, wo, out_grad, pick, klim)


def body(
    frames,
    conv_weight,
    embed_weight,
    query_weight,
    key_weight,
    value_weight,
    output_weight,
    out_grad,
    bucket_owner,
    clip_bucket,
    clip_frames,
    clip_grid,
):
    n_wide = lax.axis_size("wide")
    dp, slab = lax.axis_index("dp"), lax.axis_index("wide")
    p, c = dp // 2, dp % 2
    clips, fr, sites = frames.shape[1:4]
    buckets = bucket_owner.shape[0]
    table = (clip_bucket[:, :, None] == jnp.arange(buckets, dtype=jnp.int32)).astype(jnp.int32)
    owners = jnp.sum(table * bucket_owner, axis=-1)
    grid_tokens = clip_grid[..., 0] * clip_grid[..., 1]

    def own_parity(values):
        values = values.reshape(2, 2, clips)
        return jnp.where(c == 0, values[:, 0], values[:, 1])

    owner, live_frames, live_tokens = own_parity(owners), own_parity(clip_frames), own_parity(grid_tokens)
    key_tokens = jnp.where(live_tokens > 0, live_tokens, sites)
    site = jnp.arange(sites, dtype=jnp.int32)
    klim = (site[None, None, None, :] < key_tokens[:, :, None, None]) & jnp.ones((2, clips, fr, sites), bool)
    klim = klim.reshape(2 * clips, fr * sites).astype(F32)
    ab = jnp.arange(4, dtype=jnp.int32)
    to = ((ab // 2) ^ p) * 2 + ((ab % 2) ^ c)
    frame = slab * fr + jnp.arange(fr, dtype=jnp.int32)
    hit = to[:, None, None] == owner
    live = frame < live_frames[:, :, None]
    lanes = (hit[..., None] & live[None]).reshape(-1)
    limit = jnp.broadcast_to(live_tokens[None, :, :, None], (4, 2, clips, fr)).reshape(-1)
    pick = (lanes[None, :] & (site[:, None] < limit[None, :])).astype(BF16)
    block, grad_q, grad_k, grad_v, grad_o = run_block(
        n_wide,
        frames[0],
        conv_weight,
        embed_weight,
        query_weight,
        key_weight,
        value_weight,
        output_weight,
        out_grad[0],
        pick,
        klim,
    )
    return (block[None], *(g.astype(F32) for g in (grad_q, grad_k, grad_v, grad_o)))


def solution(mesh):
    rows = P("wide", None)
    slabs = P("dp", None, "wide", None, None)
    in_specs = (slabs, P(), P(), rows, rows, rows, rows, slabs, P(), P(), P(), P())
    out_specs = (slabs, rows, rows, rows, rows)
    return jax.shard_map(body, mesh=mesh, in_specs=in_specs, out_specs=out_specs, check_vma=False)
```

```python
import functools
import math

import jax
import jax.numpy as jnp
from jax import lax
from jax.experimental import pallas as pl
from jax.experimental.pallas import tpu as pltpu
from jax.sharding import PartitionSpec as P

HEAD_DIM = 128
MESH = pl.DeviceIdType.MESH
EPS = 1e-06
masked_score = -1e30
F32, BF16 = jnp.float32, jnp.bfloat16


def remote(src, dst, send, recv, peer):
    return pltpu.make_async_remote_copy(
        src_ref=src, dst_ref=dst, send_sem=send, recv_sem=recv, device_id=peer, device_id_type=MESH
    )


def span(start, size):
    return pl.ds(pl.multiple_of(start, 128 if size % 128 == 0 else 16), size)


def both(*conds):
    out = None
    for cond in conds:
        if cond is not None:
            out = cond if out is None else jnp.logical_and(out, cond)
    return out


def guarded(cond, action):
    if cond is None:
        action()
    else:
        pl.when(cond)(action)


def kernel(n_wide, clips, fr, sites, scale, *refs):
    frames, conv_in, embed_in, wq, wk, wv, wo, og_in, pick, klim = refs[:10]
    block_out, fin_q, fin_k, fin_v, fin_o = refs[10:15]
    (
        fbuf, conv, embed, weights, out_w, enc, tokens, normed, normed_t, og, upst, qkv, datt, datt_x, att, att_x,
        att_t, dqkv, probs, comb, y_in, term_out, term_in, keep, keep_x, from_low, from_high,
    ) = refs[15:42]
    (
        loc, halo, xw, xo, zs, zr, bs, br, os_, or_, ds, dr, es, er, gs, gr, us, ur, ps, pr, ys, yr, cs, cr, ks,
        rs, rl, rh, a_s, a_r, b_s, b_r, f_s, f_r,
    ) = refs[42:]
    levels = n_wide // 2
    in_w = (wq, wk, wv)
    fins = (fin_q, fin_k, fin_v, fin_o)
    rows, width = wq.shape
    quarter = width // 4
    span_levels = levels // 4
    own = clips * fr * sites
    pair = fr * sites
    total = 4 * own
    channels = embed_in.shape[0]
    heads = quarter // HEAD_DIM

    dp, wide = lax.axis_index("dp"), lax.axis_index("wide")
    p, c, z, s = dp // 2, dp % 2, wide // 2, wide % 2
    j = 2 * s + p

    def dev(p_, c_, z_, s_):
        return (p_ * 2 + c_, z_ * 2 + s_)

    sib, acr, mix = dev(p, 1 - c, z, s), dev(1 - p, c, z, s), dev(1 - p, 1 - c, z, s)
    bes, diag = dev(p, c, z, 1 - s), dev(1 - p, c, z, 1 - s)
    above, below = dev(p, c, z + 1, s), dev(p, c, z - 1, s)
    low, high = z > 0, z < levels - 1
    first, last = wide == 0, wide == n_wide - 1
    primary, other = c == s, c != s
    jz, lz = z // span_levels, z % span_levels
    peers = (None, sib, acr, mix)

    pend = []

    def go(cond, copy):
        guarded(cond, copy.start)
        pend.append((cond, copy))

    def arrive(cond, view, sem):
        guarded(cond, remote(view, view, sem, sem, sib).wait_recv)

    barrier = pltpu.get_barrier_semaphore()

    def greet(peer):
        pl.semaphore_signal(barrier, inc=1, device_id=peer, device_id_type=MESH)

    for peer in (sib, acr, mix, bes, diag):
        greet(peer)
    pl.when(high)(lambda: greet(above))
    pl.when(low)(lambda: greet(below))
    far_next, far_prev = both(s == 1, high), both(s == 0, low)
    pl.when(far_next)(lambda: greet((dp, wide + 1)))
    pl.when(far_prev)(lambda: greet((dp, wide - 1)))
    count = 5 + jnp.where(high, 1, 0) + jnp.where(low, 1, 0)
    count = count + jnp.where(s == 1, jnp.where(high, 1, 0), jnp.where(low, 1, 0))

    def shard(level, side):
        return span((level * 2 + side) * rows, rows)

    def quart(k):
        return span(k * quarter, quarter)

    locals_ = [
        pltpu.make_async_copy(frames, fbuf.at[:, pl.ds(fr, fr)], loc.at[0]),
        pltpu.make_async_copy(conv_in, conv, loc.at[1]),
        pltpu.make_async_copy(embed_in, embed, loc.at[2]),
    ]
    locals_ += [
        pltpu.make_async_copy(in_w[m].at[:, quart(j)], weights.at[m, shard(z, s)], loc.at[3 + m]) for m in range(3)
    ]
    own_og = [pltpu.make_async_copy(og_in.at[g * 2 + c], og.at[0, g], loc.at[6 + g]) for g in range(2)]
    own_o = pltpu.make_async_copy(wo, out_w.at[0, shard(lz, s)], loc.at[8])
    at_source = j == jz
    for copy in locals_ + own_og:
        copy.start()
    pl.when(at_source)(own_o.start)

    @pl.when(first)
    def _():
        fbuf[:, 0:fr] = jnp.zeros((clips, fr, sites, channels), BF16)

    pl.semaphore_wait(barrier, count)

    go(
        jnp.logical_not(last),
        remote(frames, fbuf.at[:, pl.ds(0, fr)], halo.at[0], halo.at[1], (dp, wide + 1)),
    )
    j_bes = 2 * (1 - s) + p
    for m in range(3):
        go(primary, remote(in_w[m].at[:, quart(j_bes)], weights.at[m, shard(z, s)], xw.at[0, m], xw.at[1, m], bes))

    def z_start(m):
        locals_[3 + m].wait()
        view = weights.at[m, shard(z, c)]
        arrive(other, view, xw.at[1, m])
        go(high, remote(view, view, zs.at[m, z, 0], zr.at[m, z], above))
        go(low, remote(view, view, zs.at[m, z, 1], zr.at[m, z], below))
        go(other, remote(view, view, bs.at[m, z], br.at[m, z], sib))

    def z_step(m, t):
        for down in range(2):
            valid = z + t <= levels - 1 if down else z >= t
            i = jnp.where(valid, z + t if down else z - t, z)
            view = weights.at[m, shard(i, c)]
            arrive(valid, view, zr.at[m, i])
            if t < levels - 1:
                peer = below if down else above
                go(both(valid, low if down else high), remote(view, view, zs.at[m, i, down], zr.at[m, i], peer))
            go(valid, remote(view, view, bs.at[m, i], br.at[m, i], sib))

    def z_done(m):
        for i in range(levels):
            arrive(jnp.logical_or(z != i, primary), weights.at[m, shard(i, 1 - c)], br.at[m, i])

    def o_view(q, i, side):
        return out_w.at[q, shard(i // 4, side), span((i % 4) * quarter, quarter)]

    def o_start():
        pl.when(at_source)(own_o.wait)
        arrive(both(at_source, other), out_w.at[0, shard(lz, c)], xo.at[1])
        for i in range(levels):
            here, view = z == j * span_levels + i // 4, o_view(0, i, c)
            go(both(here, high), remote(view, view, zs.at[3, i, 0], zr.at[3, i], above))
            go(both(here, low), remote(view, view, zs.at[3, i, 1], zr.at[3, i], below))
            go(here, remote(view, o_view(1, i, c), os_.at[i], or_.at[i], bes))
            go(both(here, other), remote(view, view, bs.at[3, i], br.at[3, i], sib))

    def o_step(i):
        source = j * span_levels + i // 4
        view, away = o_view(0, i, c), z != source
        arrive(away, view, zr.at[3, i])
        go(both(z > source, high), remote(view, view, zs.at[3, i, 0], zr.at[3, i], above))
        go(both(z < source, low), remote(view, view, zs.at[3, i, 1], zr.at[3, i], below))
        go(away, remote(view, o_view(1, i, c), os_.at[i], or_.at[i], bes))
        go(away, remote(view, view, bs.at[3, i], br.at[3, i], sib))

    def o_cross(i):
        view = o_view(1, i, c)
        arrive(None, view, or_.at[i])
        go(None, remote(view, view, ds.at[i], dr.at[i], sib))

    def o_done():
        for i in range(levels):
            source = j * span_levels + i // 4
            arrive(jnp.logical_or(z != source, primary), o_view(0, i, 1 - c), br.at[3, i])
            arrive(None, o_view(1, i, 1 - c), dr.at[i])

    def encode():
        arrive(jnp.logical_not(first), fbuf.at[:, pl.ds(0, fr)], halo.at[1])
        locals_[0].wait()
        locals_[1].wait()
        for clip in range(clips):
            raw = fbuf[clip].astype(F32)
            active = (raw / (1.0 + jnp.exp(-raw))).astype(BF16)
            acc = raw[fr:].reshape(pair, channels)
            for tap in range(3):
                moved = active[fr - tap : 2 * fr - tap].reshape(pair, channels)
                acc = acc + jnp.dot(moved, conv[tap], preferred_element_type=F32)
            enc[j, pl.ds(clip * pair, pair)] = acc.astype(BF16)
        for k, peer in enumerate((acr, bes, diag)):
            go(None, remote(enc.at[j], enc.at[j], es.at[k], er.at[k], peer))

    def embed_block(k):
        p_ = 1 - p if k in (1, 3) else p
        s_ = 1 - s if k in (2, 3) else s
        jb = 2 * s_ + p_
        if k:
            arrive(None, enc.at[jb], er.at[k - 1])
        else:
            locals_[2].wait()

        @pl.loop(0, own // pair)
        def _(i):
            at = span(i * pair, pair)
            token = jnp.dot(enc[jb, at], embed[...], preferred_element_type=F32).astype(BF16)
            if k < 2:
                tokens[span(p_ * own + i * pair, pair)] = token
            floats = token.astype(F32)
            center = floats - jnp.mean(floats, axis=-1, keepdims=True)
            spread = jnp.mean(center * center, axis=-1, keepdims=True)
            norm = (center * lax.rsqrt(spread + EPS)).astype(BF16)
            where = span(jb * own + i * pair, pair)
            normed[where] = norm
            turned = norm.T
            for k_ in range(n_wide):
                normed_t[k_ % 2, pl.ds(k_ // 2 * rows, rows), where] = turned[k_ * rows : (k_ + 1) * rows]

    def lane(ab, g, clip, f):
        return pick[:, pl.ds(((ab * 2 + g) * clips + clip) * fr + f, 1)]

    def og_send(g, f):
        for ab in range(1, 4):
            target = g * 2 + (1 - c if ab % 2 else c)
            go(None, remote(og_in.at[target, f], og.at[ab, g, f], gs.at[ab, g, f], gr.at[ab, g, f], peers[ab]))

    def slab_rows(side, g, size):
        return span((side * 2 + g) * own, size)

    def select(g, f):
        for ab in range(1, 4):
            arrive(None, og.at[ab, g, f], gr.at[ab, g, f])
        if f == 0:
            own_og[g].wait()
        for clip in range(clips):
            at = pl.ds(((g * clips + clip) * fr + f) * sites, sites)

            @pl.loop(0, 4)
            def _(k):
                cols = span(k * quarter, quarter)
                value = sum(og[ab, g, f, :, cols] * lane(ab, g, clip, f) for ab in range(4))
                upst[at, cols] = value

    def project(m):
        z_done(m)

        @pl.loop(0, 2)
        def _(i):
            at = span(i * 2 * own, 2 * own)
            qkv[m, at] = jnp.dot(normed[at], weights[m], preferred_element_type=F32).astype(BF16)

    def wide_dot(x, y):
        return lax.dot_general(x, y, (((1,), (1,)), ((), ())), preferred_element_type=F32)

    def tall_dot(x, y):
        return lax.dot_general(x, y, (((0,), (0,)), ((), ())), preferred_element_type=F32)

    def score(side, g):
        @pl.loop(g * clips, (g + 1) * clips)
        def _(k):
            b = side * 2 * clips + k
            at = span(b * pair, pair)
            frame_of = lax.broadcasted_iota(jnp.int32, (pair, pair), 0) // sites
            key_of = lax.broadcasted_iota(jnp.int32, (pair, pair), 1) // sites
            valid = jnp.logical_and(frame_of == key_of, klim[pl.ds(k, 1), :] > 0)
            for h in range(heads):
                lanes = pl.ds(h * HEAD_DIM, HEAD_DIM)
                scores = jnp.where(valid, wide_dot(qkv[0, at, lanes], qkv[1, at, lanes]) * scale, masked_score)
                top = jnp.exp(scores - jnp.max(scores, axis=-1, keepdims=True))
                probs[b, h] = top * (1.0 / jnp.sum(top, axis=-1, keepdims=True))

    def attend(side):
        @pl.loop(0, 2 * clips)
        def _(k):
            b = side * 2 * clips + k
            at = span(b * pair, pair)
            for h in range(heads):
                lanes = pl.ds(h * HEAD_DIM, HEAD_DIM)
                att[at, lanes] = jnp.dot(
                    probs[b, h].astype(BF16), qkv[2, at, lanes], preferred_element_type=F32
                ).astype(BF16)

    def att_send():
        at = slab_rows(1 - s, 0, 2 * own)
        go(None, remote(att.at[at], att_x, ps.at[0], pr.at[0], bes))

    def turn(q):
        if q:
            arrive(None, att_x, pr.at[0])

        @pl.loop(0, 2 * own // pair)
        def _(i):
            to = span(i * pair, pair)
            block = att_x[to] if q else att[span(s * 2 * own + i * pair, pair)]
            turned = block.T
            for k_ in range(2 * span_levels):
                att_t[q, k_ % 2, pl.ds(k_ // 2 * rows, rows), to] = turned[k_ * rows : (k_ + 1) * rows]

    def attend_back(side, g):
        @pl.loop(g * clips, (g + 1) * clips)
        def _(k):
            b = side * 2 * clips + k
            at = span(b * pair, pair)
            for h in range(heads):
                lanes = pl.ds(h * HEAD_DIM, HEAD_DIM)
                q, k_, v, g = qkv[0, at, lanes], qkv[1, at, lanes], qkv[2, at, lanes], datt[at, lanes]
                prob = probs[b, h]
                d_probs = wide_dot(g, v)
                inner = jnp.sum(prob * d_probs, axis=-1, keepdims=True)
                d_scores = (prob * (d_probs - inner) * scale).astype(BF16)
                dqkv[0, at, lanes] = jnp.dot(d_scores, k_, preferred_element_type=F32).astype(BF16)
                dqkv[1, at, lanes] = tall_dot(d_scores, q).astype(BF16)
                dqkv[2, at, lanes] = tall_dot(prob.astype(BF16), g).astype(BF16)

    def back_project(q, g):
        at, to = pl.ds(g * own, own), slab_rows(s, g, own)
        value = wide_dot(upst[at], out_w[q]).astype(BF16)
        if q:
            datt_x[at] = value
            go(None, remote(datt_x.at[at], datt.at[to], us.at[g], ur.at[g], bes))
        else:
            datt[to] = value

    def datt_done(g):
        arrive(None, datt.at[slab_rows(1 - s, g, own)], ur.at[g])

    def combine(g):
        keep_tokens = jnp.where(p == 0, 1.0, 0.0).astype(F32)
        at, to = slab_rows(s, g, own), pl.ds(g * own, own)

        @pl.loop(0, 4)
        def _(k):
            cols = span(k * quarter, quarter)
            value = jnp.dot(att[at], out_w[0, :, cols], preferred_element_type=F32)
            value = value + jnp.dot(att_x[to], out_w[1, :, cols], preferred_element_type=F32)
            comb[to, cols] = (value + tokens[to, cols].astype(F32) * keep_tokens).astype(BF16)

    def slots(g):
        for f in range(fr):
            for ab in (3, 2, 1, 0):
                slot = og.at[ab, g, f] if ab else y_in.at[0, g, f]

                @pl.loop(0, 4)
                def _(k):
                    cols = span(k * quarter, quarter)
                    slot[:, cols] = sum(
                        comb[pl.ds(((g * clips + clip) * fr + f) * sites, sites), cols] * lane(ab, g, clip, f)
                        for clip in range(clips)
                    )

                if ab:
                    go(None, remote(slot, y_in.at[ab, g, f], ys.at[ab, g, f], yr.at[ab, g, f], peers[ab]))

    def finish_out(g):
        for f in range(fr):
            for ab in range(1, 4):
                arrive(None, y_in.at[ab, g, f], yr.at[ab, g, f])
            for b in range(2):
                target = g * 2 + (1 - c if b else c)
                block_out[target, f] = (y_in[b, g, f].astype(F32) + y_in[2 + b, g, f].astype(F32)).astype(BF16)

    def message(m, i):
        return span(i * rows, rows)

    def terms(m, side, put):
        if m < 3:

            @pl.loop(0, 2)
            def _(i):
                at = span(i * (width // 4), width // 4)
                put(at, jnp.dot(normed_t[side, at], dqkv[m], preferred_element_type=F32))
        else:

            @pl.loop(0, 4)
            def _(piece):
                cols = span(piece * quarter, quarter)
                value = jnp.dot(att_t[m - 3, side], upst[:, cols], preferred_element_type=F32)
                for k in range(span_levels):
                    put(span((k * 4 + piece) * rows, rows), value[k * rows : (k + 1) * rows])

    def emit(m):
        def put(at, value):
            term_out[m, at] = value.astype(BF16)

        terms(m, 1 - c, put)
        go(None, remote(term_out.at[m], term_in.at[m], cs.at[m], cr.at[m], sib))

    def fold(m):
        arrive(None, term_in.at[m], cr.at[m])
        if m == 3:
            arrive(None, keep_x, ks.at[1])

        def put(at, value):
            value = value + term_in[m, at].astype(F32)
            if m == 3:
                value = value + keep_x[at].astype(F32)
            keep[m, at] = value.astype(BF16)

        terms(m, c, put)
        if m == 4:
            go(None, remote(keep.at[4], keep_x, ks.at[0], ks.at[1], bes))

    def target(m, i):
        return i if m < 3 else j * span_levels + i // 4

    def add_in(m, i, source, sem):
        at = message(m, i)
        arrive(None, source.at[m, at], sem.at[m, i])
        keep[m, at] = (keep[m, at].astype(F32) + source[m, at].astype(F32)).astype(BF16)

    def pass_on(m, *ks):
        for k in ks:
            for part in range(levels * k // 4, levels * (k + 1) // 4):
                pass_one(m, part)

    def pass_one(m, k):
        i = jnp.where(z < levels // 2, levels - 1 - k, k) if m < 3 else k
        d = target(m, i)
        upward, downward = z < d, z > d
        pl.when(both(upward, low))(lambda: add_in(m, i, from_low, rl))
        pl.when(both(downward, high))(lambda: add_in(m, i, from_high, rh))
        at = message(m, i)
        view = keep.at[m, at]
        go(upward, remote(view, from_low.at[m, at], rs.at[m, i], rl.at[m, i], above))
        go(downward, remote(view, from_high.at[m, at], rs.at[m, i], rh.at[m, i], below))

    def settle(m):
        fin = fins[m]
        if m < 3:
            pl.when(low)(lambda: add_in(m, z, from_low, rl))
            pl.when(high)(lambda: add_in(m, z, from_high, rh))
            view, place = keep.at[m, message(m, z)], fin.at[:, quart(j)]
            go(other, remote(view, place, a_s.at[m, 0], a_r.at[m, 0], bes))

            @pl.when(primary)
            def _():
                fin[:, quart(j)] = keep[m, message(m, z)]

            go(primary, remote(view, place, b_s.at[m, 0], b_r.at[m, 0], acr))
        else:
            for piece in range(4):
                i = lz * 4 + piece
                cols = pl.ds(piece * quarter, quarter)
                pl.when(both(at_source, low))(lambda: add_in(m, i, from_low, rl))
                pl.when(both(at_source, high))(lambda: add_in(m, i, from_high, rh))
                go(
                    both(at_source, other),
                    remote(keep.at[m, message(m, i)], fin.at[:, cols], a_s.at[m, piece], a_r.at[m, piece], bes),
                )

                @pl.when(both(at_source, primary))
                def _():
                    fin[:, cols] = keep[m, message(m, i)]

    def spread(m):
        fin = fins[m]
        if m < 3:
            place = fin.at[:, quart(j_bes)]
            arrive(primary, place, a_r.at[m, 0])
            go(primary, remote(place, place, b_s.at[m, 1], b_r.at[m, 1], acr))
        else:
            p_z = jz % 2
            for piece in range(4):
                place = fin.at[:, pl.ds(piece * quarter, quarter)]
                arrive(both(primary, j_bes == jz), place, a_r.at[m, piece])
                go(both(primary, p == p_z), remote(place, place, b_s.at[m, piece], b_r.at[m, piece], acr))

    def share(m):
        fin = fins[m]
        if m < 3:
            for k, side in enumerate((s, 1 - s)):
                arrive(primary, fin.at[:, quart(2 * side + 1 - p)], b_r.at[m, k])
        else:
            for piece in range(4):
                place = fin.at[:, pl.ds(piece * quarter, quarter)]
                arrive(both(primary, p != jz % 2), place, b_r.at[m, piece])
        go(primary, remote(fin, fin, f_s.at[m], f_r.at[m], sib))

    def complete(m):
        arrive(other, fins[m], f_r.at[m])

    pieces = [(g, f) for g in range(2) for f in range(fr)]
    steps = [(t, m) for t in range(1, levels) for m in range(2)]
    done = [0]

    def advance(k):
        while done[0] < len(steps) * k // 6:
            t, m = steps[done[0]]
            z_step(m, t)
            done[0] += 1

    def v_steps(k):
        for t in range(1 + (levels - 1) * k // 3, 1 + (levels - 1) * (k + 1) // 3):
            z_step(2, t)

    z_start(0)
    og_send(*pieces[0])
    encode()
    z_start(1)
    go(
        both(primary, j_bes == jz),
        remote(wo, out_w.at[0, shard(lz, s)], xo.at[0], xo.at[1], bes),
    )
    for piece in pieces[1:]:
        og_send(*piece)

    def o_steps(k):
        for i in range(levels * k // 4, levels * (k + 1) // 4):
            o_step(i)

    def o_crosses(k):
        for i in range(levels * k // 4, levels * (k + 1) // 4):
            o_cross(i)

    embed_block(0)
    advance(1)
    o_start()
    z_start(2)
    embed_block(1)
    advance(2)
    embed_block(2)
    advance(3)
    select(*pieces[0])
    advance(4)
    embed_block(3)
    advance(6)
    project(0)
    select(*pieces[1])
    o_steps(0)
    project(1)
    o_steps(1)
    o_crosses(0)
    score(1 - s, 0)
    o_steps(2)
    v_steps(0)
    o_crosses(1)
    score(1 - s, 1)
    o_steps(3)
    o_crosses(2)
    select(*pieces[2])
    score(s, 0)
    o_crosses(3)
    v_steps(1)
    o_done()
    back_project(1, 0)
    back_project(0, 0)
    score(s, 1)
    v_steps(2)
    for piece in pieces[3:]:
        select(*piece)
    back_project(1, 1)
    project(2)
    attend(1 - s)
    att_send()
    back_project(0, 1)
    attend(s)
    attend_back(s, 0)
    attend_back(s, 1)
    turn(0)
    datt_done(0)
    attend_back(1 - s, 0)
    datt_done(1)
    attend_back(1 - s, 1)
    emit(2)
    emit(1)
    fold(2)
    pass_on(2, 0)
    fold(1)
    turn(1)
    pass_on(2, 1)
    emit(4)
    pass_on(2, 2)
    combine(0)
    pass_on(2, 3)
    slots(0)
    fold(4)
    pass_on(1, 0)
    emit(0)
    emit(3)
    pass_on(1, 1)
    combine(1)
    pass_on(1, 2)
    slots(1)
    pass_on(1, 3)
    settle(2)
    fold(0)
    fold(3)
    pass_on(3, 0, 1)
    spread(2)
    pass_on(3, 2, 3)
    settle(1)
    share(2)
    pass_on(0, 0, 1)
    spread(1)
    settle(3)
    pass_on(0, 2, 3)
    share(1)
    spread(3)
    finish_out(0)
    settle(0)
    share(3)
    spread(0)
    finish_out(1)
    share(0)
    for m in (3, 2, 1, 0):
        complete(m)
    for cond, copy in pend:
        guarded(cond, copy.wait_send)


def run_block(n_wide, frames, conv_w, embed_w, wq, wk, wv, wo, out_grad, pick, klim):
    clips, fr, sites, channels = frames.shape
    rows, width = wq.shape
    quarter, levels = width // 4, n_wide // 2
    own, pair = clips * fr * sites, fr * sites
    total = 4 * own
    heads = quarter // HEAD_DIM
    dma = pltpu.SemaphoreType.DMA
    anywhere = pl.BlockSpec(memory_space=pl.ANY)
    vmem = pl.BlockSpec(memory_space=pltpu.VMEM)

    def buf(*shape, dtype=BF16):
        return pltpu.VMEM(shape, dtype)

    reach = levels * rows
    scratch = [
        buf(clips, 2 * fr, sites, channels),
        buf(3, channels, channels),
        buf(channels, width),
        buf(3, width, quarter),
        buf(2, quarter, width),
        buf(4, own, channels),
        buf(2 * own, width),
        buf(total, width),
        buf(2, width // 2, total),
        buf(4, 2, fr, sites, width),
        buf(2 * own, width),
        buf(3, total, quarter),
        buf(total, quarter),
        buf(2 * own, quarter),
        buf(total, quarter),
        buf(2 * own, quarter),
        buf(2, 2, quarter // 2, 2 * own),
        buf(3, total, quarter),
        buf(total // pair, heads, pair, pair, dtype=F32),
        buf(2 * own, width),
        buf(4, 2, fr, sites, width),
        buf(5, reach, quarter),
        buf(5, reach, quarter),
        buf(5, reach, quarter),
        buf(reach, quarter),
        buf(4, reach, quarter),
        buf(4, reach, quarter),
        dma((9,)),
        dma((2,)),
        dma((2, 3)),
        dma((2,)),
        dma((4, levels, 2)),
        dma((4, levels)),
        dma((4, levels)),
        dma((4, levels)),
        *([dma((levels,))] * 4),
        dma((3,)),
        dma((3,)),
        dma((4, 2, fr)),
        dma((4, 2, fr)),
        *([dma((2,))] * 4),
        dma((4, 2, fr)),
        dma((4, 2, fr)),
        dma((5,)),
        dma((5,)),
        dma((2,)),
        dma((4, levels)),
        dma((4, levels)),
        dma((4, levels)),
        *([dma((4, 4))] * 4),
        dma((4,)),
        dma((4,)),
    ]
    return pl.pallas_call(
        functools.partial(kernel, n_wide, clips, fr, sites, 1.0 / math.sqrt(HEAD_DIM)),
        out_shape=[jax.ShapeDtypeStruct(out_grad.shape, BF16)]
        + [jax.ShapeDtypeStruct((rows, width), BF16)] * 4,
        in_specs=[anywhere] * 8 + [vmem] * 2,
        out_specs=[vmem] * 5,
        scratch_shapes=scratch,
        compiler_params=pltpu.CompilerParams(
            collective_id=0, has_side_effects=True, vmem_limit_bytes=63 * 1024 * 1024
        ),
        cost_estimate=pl.CostEstimate(flops=12_000_000_000, bytes_accessed=20_000_000, transcendentals=0),
        name="section",
    )(frames, conv_w, embed_w, wq, wk, wv, wo, out_grad, pick, klim)


def body(
    frames,
    conv_weight,
    embed_weight,
    query_weight,
    key_weight,
    value_weight,
    output_weight,
    out_grad,
    bucket_owner,
    clip_bucket,
    clip_frames,
    clip_grid,
):
    n_wide = lax.axis_size("wide")
    dp, slab = lax.axis_index("dp"), lax.axis_index("wide")
    p, c = dp // 2, dp % 2
    clips, fr, sites = frames.shape[1:4]
    buckets = bucket_owner.shape[0]
    table = (clip_bucket[:, :, None] == jnp.arange(buckets, dtype=jnp.int32)).astype(jnp.int32)
    owners = jnp.sum(table * bucket_owner, axis=-1)
    grid_tokens = clip_grid[..., 0] * clip_grid[..., 1]

    def own_parity(values):
        values = values.reshape(2, 2, clips)
        return jnp.where(c == 0, values[:, 0], values[:, 1])

    owner, live_frames, live_tokens = own_parity(owners), own_parity(clip_frames), own_parity(grid_tokens)
    key_tokens = jnp.where(live_tokens > 0, live_tokens, sites)
    site = jnp.arange(sites, dtype=jnp.int32)
    klim = (site[None, None, None, :] < key_tokens[:, :, None, None]) & jnp.ones((2, clips, fr, sites), bool)
    klim = klim.reshape(2 * clips, fr * sites).astype(F32)
    ab = jnp.arange(4, dtype=jnp.int32)
    to = ((ab // 2) ^ p) * 2 + ((ab % 2) ^ c)
    frame = slab * fr + jnp.arange(fr, dtype=jnp.int32)
    hit = to[:, None, None] == owner
    live = frame < live_frames[:, :, None]
    lanes = (hit[..., None] & live[None]).reshape(-1)
    limit = jnp.broadcast_to(live_tokens[None, :, :, None], (4, 2, clips, fr)).reshape(-1)
    pick = (lanes[None, :] & (site[:, None] < limit[None, :])).astype(BF16)
    block, grad_q, grad_k, grad_v, grad_o = run_block(
        n_wide,
        frames[0],
        conv_weight,
        embed_weight,
        query_weight,
        key_weight,
        value_weight,
        output_weight,
        out_grad[0],
        pick,
        klim,
    )
    return (block[None], *(g.astype(F32) for g in (grad_q, grad_k, grad_v, grad_o)))


def solution(mesh):
    rows = P("wide", None)
    slabs = P("dp", None, "wide", None, None)
    in_specs = (slabs, P(), P(), rows, rows, rows, rows, slabs, P(), P(), P(), P())
    out_specs = (slabs, rows, rows, rows, rows)
    return jax.shard_map(body, mesh=mesh, in_specs=in_specs, out_specs=out_specs, check_vma=False)
```

```python
import functools
import math

import jax
import jax.numpy as jnp
from jax import lax
from jax.experimental import pallas as pl
from jax.experimental.pallas import tpu as pltpu
from jax.sharding import PartitionSpec as P

HEAD_DIM = 128
MESH = pl.DeviceIdType.MESH
EPS = 1e-06
masked_score = -1e30
F32, BF16 = jnp.float32, jnp.bfloat16


def remote(src, dst, send, recv, peer):
    return pltpu.make_async_remote_copy(
        src_ref=src, dst_ref=dst, send_sem=send, recv_sem=recv, device_id=peer, device_id_type=MESH
    )


def span(start, size):
    return pl.ds(pl.multiple_of(start, 128 if size % 128 == 0 else 16), size)


def both(*conds):
    out = None
    for cond in conds:
        if cond is not None:
            out = cond if out is None else jnp.logical_and(out, cond)
    return out


def guarded(cond, action):
    if cond is None:
        action()
    else:
        pl.when(cond)(action)


def kernel(n_wide, clips, fr, sites, scale, *refs):
    frames, conv_in, embed_in, wq, wk, wv, wo, og_in, pick, klim = refs[:10]
    block_out, fin_q, fin_k, fin_v, fin_o = refs[10:15]
    (
        fbuf, conv, embed, weights, out_w, enc, tokens, normed, normed_t, og, upst, qkv, datt, datt_x, att, att_x,
        att_t, dqkv, probs, comb, y_in, term_out, term_in, keep, keep_x, from_low, from_high,
    ) = refs[15:42]
    (
        loc, halo, xw, xo, zs, zr, bs, br, os_, or_, ds, dr, es, er, gs, gr, us, ur, ps, pr, ys, yr, cs, cr, ks,
        rs, rl, rh, a_s, a_r, b_s, b_r, f_s, f_r,
    ) = refs[42:]
    levels = n_wide // 2
    in_w = (wq, wk, wv)
    fins = (fin_q, fin_k, fin_v, fin_o)
    rows, width = wq.shape
    quarter = width // 4
    span_levels = levels // 4
    own = clips * fr * sites
    pair = fr * sites
    total = 4 * own
    channels = embed_in.shape[0]
    heads = quarter // HEAD_DIM

    dp, wide = lax.axis_index("dp"), lax.axis_index("wide")
    p, c, z, s = dp // 2, dp % 2, wide // 2, wide % 2
    j = 2 * s + p

    def dev(p_, c_, z_, s_):
        return (p_ * 2 + c_, z_ * 2 + s_)

    sib, acr, mix = dev(p, 1 - c, z, s), dev(1 - p, c, z, s), dev(1 - p, 1 - c, z, s)
    bes, diag = dev(p, c, z, 1 - s), dev(1 - p, c, z, 1 - s)
    above, below = dev(p, c, z + 1, s), dev(p, c, z - 1, s)
    low, high = z > 0, z < levels - 1
    first, last = wide == 0, wide == n_wide - 1
    primary, other = c == s, c != s
    jz, lz = z // span_levels, z % span_levels
    peers = (None, sib, acr, mix)

    pend = []

    def go(cond, copy):
        guarded(cond, copy.start)
        pend.append((cond, copy))

    def arrive(cond, view, sem):
        guarded(cond, remote(view, view, sem, sem, sib).wait_recv)

    barrier = pltpu.get_barrier_semaphore()

    def greet(peer):
        pl.semaphore_signal(barrier, inc=1, device_id=peer, device_id_type=MESH)

    for peer in (sib, acr, mix, bes, diag):
        greet(peer)
    pl.when(high)(lambda: greet(above))
    pl.when(low)(lambda: greet(below))
    far_next, far_prev = both(s == 1, high), both(s == 0, low)
    pl.when(far_next)(lambda: greet((dp, wide + 1)))
    pl.when(far_prev)(lambda: greet((dp, wide - 1)))
    count = 5 + jnp.where(high, 1, 0) + jnp.where(low, 1, 0)
    count = count + jnp.where(s == 1, jnp.where(high, 1, 0), jnp.where(low, 1, 0))

    def shard(level, side):
        return span((level * 2 + side) * rows, rows)

    def quart(k):
        return span(k * quarter, quarter)

    locals_ = [
        pltpu.make_async_copy(frames, fbuf.at[:, pl.ds(fr, fr)], loc.at[0]),
        pltpu.make_async_copy(conv_in, conv, loc.at[1]),
        pltpu.make_async_copy(embed_in, embed, loc.at[2]),
    ]
    locals_ += [
        pltpu.make_async_copy(in_w[m].at[:, quart(j)], weights.at[m, shard(z, s)], loc.at[3 + m]) for m in range(3)
    ]
    own_og = [pltpu.make_async_copy(og_in.at[g * 2 + c], og.at[0, g], loc.at[6 + g]) for g in range(2)]
    own_o = pltpu.make_async_copy(wo, out_w.at[0, shard(lz, s)], loc.at[8])
    at_source = j == jz
    for copy in locals_ + own_og:
        copy.start()
    pl.when(at_source)(own_o.start)

    @pl.when(first)
    def _():
        fbuf[:, 0:fr] = jnp.zeros((clips, fr, sites, channels), BF16)

    pl.semaphore_wait(barrier, count)

    go(
        jnp.logical_not(last),
        remote(frames, fbuf.at[:, pl.ds(0, fr)], halo.at[0], halo.at[1], (dp, wide + 1)),
    )
    j_bes = 2 * (1 - s) + p
    for m in (0, 1, 3, 2):
        for piece in range(4):
            cols = pl.ds(piece * quarter, quarter)
            if m == 3:
                view = out_w.at[0, shard(lz, s), cols]
                go(both(primary, j_bes == jz), remote(wo.at[:, cols], view, xo.at[0, piece], xo.at[1, piece], bes))
        if m < 3:
            view = weights.at[m, shard(z, s)]
            go(primary, remote(in_w[m].at[:, quart(j_bes)], view, xw.at[0, m], xw.at[1, m], bes))

    def z_start(m):
        locals_[3 + m].wait()
        view = weights.at[m, shard(z, c)]
        arrive(other, view, xw.at[1, m])
        go(high, remote(view, view, zs.at[m, z, 0], zr.at[m, z], above))
        go(low, remote(view, view, zs.at[m, z, 1], zr.at[m, z], below))
        go(other, remote(view, view, bs.at[m, z], br.at[m, z], sib))

    def z_step(m, t):
        for down in range(2):
            valid = z + t <= levels - 1 if down else z >= t
            i = jnp.where(valid, z + t if down else z - t, z)
            view = weights.at[m, shard(i, c)]
            arrive(valid, view, zr.at[m, i])
            if t < levels - 1:
                peer = below if down else above
                go(both(valid, low if down else high), remote(view, view, zs.at[m, i, down], zr.at[m, i], peer))
            go(valid, remote(view, view, bs.at[m, i], br.at[m, i], sib))

    def z_done(m):
        for i in range(levels):
            arrive(jnp.logical_or(z != i, primary), weights.at[m, shard(i, 1 - c)], br.at[m, i])

    def o_view(q, i, side):
        return out_w.at[q, shard(i // 4, side), span((i % 4) * quarter, quarter)]

    def o_start(k):
        if k == 0:
            pl.when(at_source)(own_o.wait)
        for i in range(levels * k // 4, levels * (k + 1) // 4):
            here, view = z == j * span_levels + i // 4, o_view(0, i, c)
            arrive(both(here, other), view, xo.at[1, i % 4])
            go(both(here, high), remote(view, view, zs.at[3, i, 0], zr.at[3, i], above))
            go(both(here, low), remote(view, view, zs.at[3, i, 1], zr.at[3, i], below))
            go(here, remote(view, o_view(1, i, c), os_.at[i], or_.at[i], bes))
            go(both(here, other), remote(view, view, bs.at[3, i], br.at[3, i], sib))

    def o_step(i):
        source = j * span_levels + i // 4
        view, away = o_view(0, i, c), z != source
        arrive(away, view, zr.at[3, i])
        go(both(z > source, high), remote(view, view, zs.at[3, i, 0], zr.at[3, i], above))
        go(both(z < source, low), remote(view, view, zs.at[3, i, 1], zr.at[3, i], below))
        go(away, remote(view, o_view(1, i, c), os_.at[i], or_.at[i], bes))
        go(away, remote(view, view, bs.at[3, i], br.at[3, i], sib))

    def o_cross(i):
        view = o_view(1, i, c)
        arrive(None, view, or_.at[i])
        go(None, remote(view, view, ds.at[i], dr.at[i], sib))

    def o_done():
        for i in range(levels):
            source = j * span_levels + i // 4
            arrive(jnp.logical_or(z != source, primary), o_view(0, i, 1 - c), br.at[3, i])
            arrive(None, o_view(1, i, 1 - c), dr.at[i])

    def encode():
        arrive(jnp.logical_not(first), fbuf.at[:, pl.ds(0, fr)], halo.at[1])
        locals_[0].wait()
        locals_[1].wait()
        for clip in range(clips):
            raw = fbuf[clip].astype(F32)
            active = (raw / (1.0 + jnp.exp(-raw))).astype(BF16)
            acc = raw[fr:].reshape(pair, channels)
            for tap in range(3):
                moved = active[fr - tap : 2 * fr - tap].reshape(pair, channels)
                acc = acc + jnp.dot(moved, conv[tap], preferred_element_type=F32)
            enc[j, pl.ds(clip * pair, pair)] = acc.astype(BF16)
        for k, peer in enumerate((acr, bes, diag)):
            go(None, remote(enc.at[j], enc.at[j], es.at[k], er.at[k], peer))

    def embed_block(k):
        p_ = 1 - p if k in (1, 3) else p
        s_ = 1 - s if k in (2, 3) else s
        jb = 2 * s_ + p_
        if k:
            arrive(None, enc.at[jb], er.at[k - 1])
        else:
            locals_[2].wait()

        @pl.loop(0, own // pair)
        def _(i):
            at = span(i * pair, pair)
            token = jnp.dot(enc[jb, at], embed[...], preferred_element_type=F32).astype(BF16)
            if k < 2:
                tokens[span(p_ * own + i * pair, pair)] = token
            floats = token.astype(F32)
            center = floats - jnp.mean(floats, axis=-1, keepdims=True)
            spread = jnp.mean(center * center, axis=-1, keepdims=True)
            norm = (center * lax.rsqrt(spread + EPS)).astype(BF16)
            where = span(jb * own + i * pair, pair)
            normed[where] = norm
            turned = norm.T
            for k_ in range(n_wide):
                normed_t[k_ % 2, pl.ds(k_ // 2 * rows, rows), where] = turned[k_ * rows : (k_ + 1) * rows]

    def lane(ab, g, clip, f):
        return pick[:, pl.ds(((ab * 2 + g) * clips + clip) * fr + f, 1)]

    def og_send(g, f):
        for ab in range(1, 4):
            target = g * 2 + (1 - c if ab % 2 else c)
            go(None, remote(og_in.at[target, f], og.at[ab, g, f], gs.at[ab, g, f], gr.at[ab, g, f], peers[ab]))

    def slab_rows(side, g, size):
        return span((side * 2 + g) * own, size)

    def select(g, f):
        for ab in range(1, 4):
            arrive(None, og.at[ab, g, f], gr.at[ab, g, f])
        if f == 0:
            own_og[g].wait()
        for clip in range(clips):
            at = pl.ds(((g * clips + clip) * fr + f) * sites, sites)

            @pl.loop(0, 4)
            def _(k):
                cols = span(k * quarter, quarter)
                value = sum(og[ab, g, f, :, cols] * lane(ab, g, clip, f) for ab in range(4))
                upst[at, cols] = value

    def project(m):
        z_done(m)

        @pl.loop(0, 2)
        def _(i):
            at = span(i * 2 * own, 2 * own)
            qkv[m, at] = jnp.dot(normed[at], weights[m], preferred_element_type=F32).astype(BF16)

    def wide_dot(x, y):
        return lax.dot_general(x, y, (((1,), (1,)), ((), ())), preferred_element_type=F32)

    def tall_dot(x, y):
        return lax.dot_general(x, y, (((0,), (0,)), ((), ())), preferred_element_type=F32)

    def score(side, g):
        @pl.loop(g * clips, (g + 1) * clips)
        def _(k):
            b = side * 2 * clips + k
            at = span(b * pair, pair)
            frame_of = lax.broadcasted_iota(jnp.int32, (pair, pair), 0) // sites
            key_of = lax.broadcasted_iota(jnp.int32, (pair, pair), 1) // sites
            valid = jnp.logical_and(frame_of == key_of, klim[pl.ds(k, 1), :] > 0)
            for h in range(heads):
                lanes = pl.ds(h * HEAD_DIM, HEAD_DIM)
                scores = jnp.where(valid, wide_dot(qkv[0, at, lanes], qkv[1, at, lanes]) * scale, masked_score)
                top = jnp.exp(scores - jnp.max(scores, axis=-1, keepdims=True))
                probs[b, h] = top * (1.0 / jnp.sum(top, axis=-1, keepdims=True))

    def attend(side):
        @pl.loop(0, 2 * clips)
        def _(k):
            b = side * 2 * clips + k
            at = span(b * pair, pair)
            for h in range(heads):
                lanes = pl.ds(h * HEAD_DIM, HEAD_DIM)
                att[at, lanes] = jnp.dot(
                    probs[b, h].astype(BF16), qkv[2, at, lanes], preferred_element_type=F32
                ).astype(BF16)

    def att_send():
        at = slab_rows(1 - s, 0, 2 * own)
        go(None, remote(att.at[at], att_x, ps.at[0], pr.at[0], bes))

    def turn(q):
        if q:
            arrive(None, att_x, pr.at[0])

        @pl.loop(0, 2 * own // pair)
        def _(i):
            to = span(i * pair, pair)
            block = att_x[to] if q else att[span(s * 2 * own + i * pair, pair)]
            turned = block.T
            for k_ in range(2 * span_levels):
                att_t[q, k_ % 2, pl.ds(k_ // 2 * rows, rows), to] = turned[k_ * rows : (k_ + 1) * rows]

    def back_values(side):
        @pl.loop(0, 2 * clips)
        def _(k):
            b = side * 2 * clips + k
            at = span(b * pair, pair)
            for h in range(heads):
                lanes = pl.ds(h * HEAD_DIM, HEAD_DIM)
                dqkv[2, at, lanes] = tall_dot(probs[b, h].astype(BF16), datt[at, lanes]).astype(BF16)

    def attend_back(side, g):
        @pl.loop(g * clips, (g + 1) * clips)
        def _(k):
            b = side * 2 * clips + k
            at = span(b * pair, pair)
            for h in range(heads):
                lanes = pl.ds(h * HEAD_DIM, HEAD_DIM)
                q, k_, v, g = qkv[0, at, lanes], qkv[1, at, lanes], qkv[2, at, lanes], datt[at, lanes]
                prob = probs[b, h]
                d_probs = wide_dot(g, v)
                inner = jnp.sum(prob * d_probs, axis=-1, keepdims=True)
                d_scores = (prob * (d_probs - inner) * scale).astype(BF16)
                dqkv[0, at, lanes] = jnp.dot(d_scores, k_, preferred_element_type=F32).astype(BF16)
                dqkv[1, at, lanes] = tall_dot(d_scores, q).astype(BF16)

    def back_project(q, g):
        at, to = pl.ds(g * own, own), slab_rows(s, g, own)
        value = wide_dot(upst[at], out_w[q]).astype(BF16)
        if q:
            datt_x[at] = value
            go(None, remote(datt_x.at[at], datt.at[to], us.at[g], ur.at[g], bes))
        else:
            datt[to] = value

    def datt_done(g):
        arrive(None, datt.at[slab_rows(1 - s, g, own)], ur.at[g])

    def combine(g):
        keep_tokens = jnp.where(p == 0, 1.0, 0.0).astype(F32)
        at, to = slab_rows(s, g, own), pl.ds(g * own, own)

        @pl.loop(0, 4)
        def _(k):
            cols = span(k * quarter, quarter)
            value = jnp.dot(att[at], out_w[0, :, cols], preferred_element_type=F32)
            value = value + jnp.dot(att_x[to], out_w[1, :, cols], preferred_element_type=F32)
            comb[to, cols] = (value + tokens[to, cols].astype(F32) * keep_tokens).astype(BF16)

    def slots(g):
        for f in range(fr):
            for ab in (3, 2, 1, 0):
                slot = og.at[ab, g, f] if ab else y_in.at[0, g, f]

                @pl.loop(0, 4)
                def _(k):
                    cols = span(k * quarter, quarter)
                    slot[:, cols] = sum(
                        comb[pl.ds(((g * clips + clip) * fr + f) * sites, sites), cols] * lane(ab, g, clip, f)
                        for clip in range(clips)
                    )

                if ab:
                    go(None, remote(slot, y_in.at[ab, g, f], ys.at[ab, g, f], yr.at[ab, g, f], peers[ab]))

    def finish_out(g):
        for f in range(fr):
            for ab in range(1, 4):
                arrive(None, y_in.at[ab, g, f], yr.at[ab, g, f])
            for b in range(2):
                target = g * 2 + (1 - c if b else c)
                block_out[target, f] = (y_in[b, g, f].astype(F32) + y_in[2 + b, g, f].astype(F32)).astype(BF16)

    def message(m, i):
        return span(i * rows, rows)

    def terms(m, side, put):
        if m < 3:

            @pl.loop(0, 2)
            def _(i):
                at = span(i * (width // 4), width // 4)
                put(at, jnp.dot(normed_t[side, at], dqkv[m], preferred_element_type=F32))
        else:

            @pl.loop(0, 4)
            def _(piece):
                cols = span(piece * quarter, quarter)
                value = jnp.dot(att_t[m - 3, side], upst[:, cols], preferred_element_type=F32)
                for k in range(span_levels):
                    put(span((k * 4 + piece) * rows, rows), value[k * rows : (k + 1) * rows])

    def emit(m):
        def put(at, value):
            term_out[m, at] = value.astype(BF16)

        terms(m, 1 - c, put)
        go(None, remote(term_out.at[m], term_in.at[m], cs.at[m], cr.at[m], sib))

    def fold(m):
        arrive(None, term_in.at[m], cr.at[m])
        if m == 3:
            arrive(None, keep_x, ks.at[1])

        def put(at, value):
            value = value + term_in[m, at].astype(F32)
            if m == 3:
                value = value + keep_x[at].astype(F32)
            keep[m, at] = value.astype(BF16)

        terms(m, c, put)
        if m == 4:
            go(None, remote(keep.at[4], keep_x, ks.at[0], ks.at[1], bes))

    def target(m, i):
        return i if m < 3 else j * span_levels + i // 4

    def add_in(m, i, source, sem):
        at = message(m, i)
        arrive(None, source.at[m, at], sem.at[m, i])
        keep[m, at] = (keep[m, at].astype(F32) + source[m, at].astype(F32)).astype(BF16)

    def pass_on(m, *ks):
        for k in ks:
            for part in range(levels * k // 4, levels * (k + 1) // 4):
                pass_one(m, part)

    def pass_one(m, k):
        i = jnp.where(z < levels // 2, levels - 1 - k, k) if m < 3 else k
        d = target(m, i)
        upward, downward = z < d, z > d
        pl.when(both(upward, low))(lambda: add_in(m, i, from_low, rl))
        pl.when(both(downward, high))(lambda: add_in(m, i, from_high, rh))
        at = message(m, i)
        view = keep.at[m, at]
        go(upward, remote(view, from_low.at[m, at], rs.at[m, i], rl.at[m, i], above))
        go(downward, remote(view, from_high.at[m, at], rs.at[m, i], rh.at[m, i], below))

    def settle(m):
        fin = fins[m]
        if m < 3:
            pl.when(low)(lambda: add_in(m, z, from_low, rl))
            pl.when(high)(lambda: add_in(m, z, from_high, rh))
            view, place = keep.at[m, message(m, z)], fin.at[:, quart(j)]
            go(other, remote(view, place, a_s.at[m, 0], a_r.at[m, 0], bes))
            go(other, remote(view, place, a_s.at[m, 1], a_r.at[m, 1], diag))

            @pl.when(primary)
            def _():
                fin[:, quart(j)] = keep[m, message(m, z)]

            go(primary, remote(view, place, b_s.at[m, 0], b_r.at[m, 0], acr))
        else:
            for piece in range(4):
                i = lz * 4 + piece
                cols = pl.ds(piece * quarter, quarter)
                pl.when(both(at_source, low))(lambda: add_in(m, i, from_low, rl))
                pl.when(both(at_source, high))(lambda: add_in(m, i, from_high, rh))
                go(
                    both(at_source, other),
                    remote(keep.at[m, message(m, i)], fin.at[:, cols], a_s.at[m, piece], a_r.at[m, piece], bes),
                )

                @pl.when(both(at_source, primary))
                def _():
                    fin[:, cols] = keep[m, message(m, i)]

    def spread(m):
        fin = fins[m]
        if m == 3:
            p_z = jz % 2
            for piece in range(4):
                place = fin.at[:, pl.ds(piece * quarter, quarter)]
                arrive(both(primary, j_bes == jz), place, a_r.at[m, piece])
                go(both(primary, p == p_z), remote(place, place, b_s.at[m, piece], b_r.at[m, piece], acr))

    def share(m):
        fin = fins[m]
        if m < 3:
            arrive(primary, fin.at[:, quart(j_bes)], a_r.at[m, 0])
            arrive(primary, fin.at[:, quart(2 * (1 - s) + 1 - p)], a_r.at[m, 1])
            arrive(primary, fin.at[:, quart(2 * s + 1 - p)], b_r.at[m, 0])
        else:
            for piece in range(4):
                place = fin.at[:, pl.ds(piece * quarter, quarter)]
                arrive(both(primary, p != jz % 2), place, b_r.at[m, piece])
        go(primary, remote(fin, fin, f_s.at[m], f_r.at[m], sib))

    def complete(m):
        arrive(other, fins[m], f_r.at[m])

    pieces = [(g, f) for g in range(2) for f in range(fr)]
    steps = [(t, m) for t in range(1, levels) for m in range(2)]
    done = [0]

    def advance(k):
        while done[0] < len(steps) * k // 6:
            t, m = steps[done[0]]
            z_step(m, t)
            done[0] += 1

    def v_steps(k):
        for t in range(1 + (levels - 1) * k // 3, 1 + (levels - 1) * (k + 1) // 3):
            z_step(2, t)


    def o_steps(k):
        for i in range(levels * k // 4, levels * (k + 1) // 4):
            o_step(i)

    def o_crosses(k):
        for i in range(levels * k // 4, levels * (k + 1) // 4):
            o_cross(i)

    z_start(0)
    z_start(1)
    advance(1)
    encode()
    og_send(*pieces[0])
    og_send(*pieces[1])
    og_send(*pieces[2])
    og_send(*pieces[3])
    z_start(2)
    advance(2)
    o_start(0)
    embed_block(0)
    o_start(1)
    advance(3)
    o_start(2)
    embed_block(1)
    advance(4)
    o_start(3)
    embed_block(2)
    advance(5)
    embed_block(3)
    advance(6)
    project(0)
    o_steps(0)
    select(*pieces[0])
    project(1)
    o_steps(1)
    o_crosses(0)
    v_steps(0)
    select(*pieces[1])
    score(1 - s, 0)
    o_steps(2)
    o_crosses(1)
    score(1 - s, 1)
    o_steps(3)
    o_crosses(2)
    v_steps(1)
    score(s, 0)
    o_crosses(3)
    select(*pieces[2])
    o_done()
    back_project(1, 0)
    back_project(0, 0)
    score(s, 1)
    v_steps(2)
    project(2)
    attend(1 - s)
    select(*pieces[3])
    back_project(1, 1)
    att_send()
    back_project(0, 1)
    attend(s)
    back_values(s)
    attend_back(s, 0)
    attend_back(s, 1)
    turn(0)
    datt_done(0)
    datt_done(1)
    back_values(1 - s)
    attend_back(1 - s, 0)
    attend_back(1 - s, 1)
    emit(2)
    emit(1)
    fold(2)
    pass_on(2, 0)
    fold(1)
    turn(1)
    pass_on(2, 1)
    emit(4)
    pass_on(2, 2)
    fold(4)
    pass_on(2, 3)
    combine(0)
    pass_on(1, 0)
    slots(0)
    emit(0)
    pass_on(1, 1)
    emit(3)
    pass_on(1, 2)
    fold(0)
    pass_on(1, 3)
    settle(2)
    combine(1)
    fold(3)
    pass_on(3, 0, 1)
    slots(1)
    pass_on(3, 2, 3)
    settle(1)
    pass_on(0, 0, 1)
    share(2)
    settle(3)
    pass_on(0, 2, 3)
    spread(3)
    settle(0)
    share(1)
    share(3)
    finish_out(0)
    finish_out(1)
    share(0)
    for m in (3, 2, 1, 0):
        complete(m)
    for cond, copy in pend:
        guarded(cond, copy.wait_send)


def run_block(n_wide, frames, conv_w, embed_w, wq, wk, wv, wo, out_grad, pick, klim):
    clips, fr, sites, channels = frames.shape
    rows, width = wq.shape
    quarter, levels = width // 4, n_wide // 2
    own, pair = clips * fr * sites, fr * sites
    total = 4 * own
    heads = quarter // HEAD_DIM
    dma = pltpu.SemaphoreType.DMA
    anywhere = pl.BlockSpec(memory_space=pl.ANY)
    vmem = pl.BlockSpec(memory_space=pltpu.VMEM)

    def buf(*shape, dtype=BF16):
        return pltpu.VMEM(shape, dtype)

    reach = levels * rows
    scratch = [
        buf(clips, 2 * fr, sites, channels),
        buf(3, channels, channels),
        buf(channels, width),
        buf(3, width, quarter),
        buf(2, quarter, width),
        buf(4, own, channels),
        buf(2 * own, width),
        buf(total, width),
        buf(2, width // 2, total),
        buf(4, 2, fr, sites, width),
        buf(2 * own, width),
        buf(3, total, quarter),
        buf(total, quarter),
        buf(2 * own, quarter),
        buf(total, quarter),
        buf(2 * own, quarter),
        buf(2, 2, quarter // 2, 2 * own),
        buf(3, total, quarter),
        buf(total // pair, heads, pair, pair, dtype=F32),
        buf(2 * own, width),
        buf(4, 2, fr, sites, width),
        buf(5, reach, quarter),
        buf(5, reach, quarter),
        buf(5, reach, quarter),
        buf(reach, quarter),
        buf(4, reach, quarter),
        buf(4, reach, quarter),
        dma((9,)),
        dma((2,)),
        dma((2, 3)),
        dma((2, 4)),
        dma((4, levels, 2)),
        dma((4, levels)),
        dma((4, levels)),
        dma((4, levels)),
        *([dma((levels,))] * 4),
        dma((3,)),
        dma((3,)),
        dma((4, 2, fr)),
        dma((4, 2, fr)),
        *([dma((2,))] * 4),
        dma((4, 2, fr)),
        dma((4, 2, fr)),
        dma((5,)),
        dma((5,)),
        dma((2,)),
        dma((4, levels)),
        dma((4, levels)),
        dma((4, levels)),
        *([dma((4, 4))] * 4),
        dma((4,)),
        dma((4,)),
    ]
    return pl.pallas_call(
        functools.partial(kernel, n_wide, clips, fr, sites, 1.0 / math.sqrt(HEAD_DIM)),
        out_shape=[jax.ShapeDtypeStruct(out_grad.shape, BF16)]
        + [jax.ShapeDtypeStruct((rows, width), BF16)] * 4,
        in_specs=[anywhere] * 8 + [vmem] * 2,
        out_specs=[vmem] * 5,
        scratch_shapes=scratch,
        compiler_params=pltpu.CompilerParams(
            collective_id=0, has_side_effects=True, vmem_limit_bytes=63 * 1024 * 1024
        ),
        cost_estimate=pl.CostEstimate(flops=12_000_000_000, bytes_accessed=20_000_000, transcendentals=0),
        name="section",
    )(frames, conv_w, embed_w, wq, wk, wv, wo, out_grad, pick, klim)


def body(
    frames,
    conv_weight,
    embed_weight,
    query_weight,
    key_weight,
    value_weight,
    output_weight,
    out_grad,
    bucket_owner,
    clip_bucket,
    clip_frames,
    clip_grid,
):
    n_wide = lax.axis_size("wide")
    dp, slab = lax.axis_index("dp"), lax.axis_index("wide")
    p, c = dp // 2, dp % 2
    clips, fr, sites = frames.shape[1:4]
    buckets = bucket_owner.shape[0]
    table = (clip_bucket[:, :, None] == jnp.arange(buckets, dtype=jnp.int32)).astype(jnp.int32)
    owners = jnp.sum(table * bucket_owner, axis=-1)
    grid_tokens = clip_grid[..., 0] * clip_grid[..., 1]

    def own_parity(values):
        values = values.reshape(2, 2, clips)
        return jnp.where(c == 0, values[:, 0], values[:, 1])

    owner, live_frames, live_tokens = own_parity(owners), own_parity(clip_frames), own_parity(grid_tokens)
    key_tokens = jnp.where(live_tokens > 0, live_tokens, sites)
    site = jnp.arange(sites, dtype=jnp.int32)
    klim = (site[None, None, None, :] < key_tokens[:, :, None, None]) & jnp.ones((2, clips, fr, sites), bool)
    klim = klim.reshape(2 * clips, fr * sites).astype(F32)
    ab = jnp.arange(4, dtype=jnp.int32)
    to = ((ab // 2) ^ p) * 2 + ((ab % 2) ^ c)
    frame = slab * fr + jnp.arange(fr, dtype=jnp.int32)
    hit = to[:, None, None] == owner
    live = frame < live_frames[:, :, None]
    lanes = (hit[..., None] & live[None]).reshape(-1)
    limit = jnp.broadcast_to(live_tokens[None, :, :, None], (4, 2, clips, fr)).reshape(-1)
    pick = (lanes[None, :] & (site[:, None] < limit[None, :])).astype(BF16)
    block, grad_q, grad_k, grad_v, grad_o = run_block(
        n_wide,
        frames[0],
        conv_weight,
        embed_weight,
        query_weight,
        key_weight,
        value_weight,
        output_weight,
        out_grad[0],
        pick,
        klim,
    )
    return (block[None], *(g.astype(F32) for g in (grad_q, grad_k, grad_v, grad_o)))


def solution(mesh):
    rows = P("wide", None)
    slabs = P("dp", None, "wide", None, None)
    in_specs = (slabs, P(), P(), rows, rows, rows, rows, slabs, P(), P(), P(), P())
    out_specs = (slabs, rows, rows, rows, rows)
    return jax.shard_map(body, mesh=mesh, in_specs=in_specs, out_specs=out_specs, check_vma=False)
```

```python
import functools
import math

import jax
import jax.numpy as jnp
from jax import lax
from jax.experimental import pallas as pl
from jax.experimental.pallas import tpu as pltpu
from jax.sharding import PartitionSpec as P

HEAD_DIM = 128
MESH = pl.DeviceIdType.MESH
EPS = 1e-06
masked_score = -1e30
F32, BF16 = jnp.float32, jnp.bfloat16


def remote(src, dst, send, recv, peer):
    return pltpu.make_async_remote_copy(
        src_ref=src, dst_ref=dst, send_sem=send, recv_sem=recv, device_id=peer, device_id_type=MESH
    )


def span(start, size):
    return pl.ds(pl.multiple_of(start, 128 if size % 128 == 0 else 16), size)


def both(*conds):
    out = None
    for cond in conds:
        if cond is not None:
            out = cond if out is None else jnp.logical_and(out, cond)
    return out


def guarded(cond, action):
    if cond is None:
        action()
    else:
        pl.when(cond)(action)


def kernel(n_wide, clips, fr, sites, scale, *refs):
    frames, conv_in, embed_in, wq, wk, wv, wo, og_in, bucket_owner, clip_bucket, clip_frames, clip_grid = refs[:12]
    block_out, fin_q, fin_k, fin_v, fin_o = refs[12:17]
    (
        fbuf, conv, embed, weights, out_w, enc, tokens, normed, normed_t, og, upst, qkv, datt, datt_x, att, att_x,
        att_t, dqkv, probs, comb, y_in, term_out, term_in, keep, keep_x, from_low, from_high, pick, klim,
    ) = refs[17:46]
    (
        loc, halo, xw, xo, zs, zr, bs, br, os_, or_, ds, dr, es, er, gs, gr, us, ur, ps, pr, ys, yr, cs, cr, ks,
        rs, rl, rh, a_s, a_r, b_s, b_r, f_s, f_r,
    ) = refs[46:]
    levels = n_wide // 2
    in_w = (wq, wk, wv)
    fins = (fin_q, fin_k, fin_v, fin_o)
    rows, width = wq.shape
    quarter = width // 4
    span_levels = levels // 4
    own = clips * fr * sites
    pair = fr * sites
    total = 4 * own
    channels = embed_in.shape[0]
    heads = quarter // HEAD_DIM

    dp, wide = lax.axis_index("dp"), lax.axis_index("wide")
    p, c, z, s = dp // 2, dp % 2, wide // 2, wide % 2
    j = 2 * s + p

    def dev(p_, c_, z_, s_):
        return (p_ * 2 + c_, z_ * 2 + s_)

    sib, acr, mix = dev(p, 1 - c, z, s), dev(1 - p, c, z, s), dev(1 - p, 1 - c, z, s)
    bes, diag = dev(p, c, z, 1 - s), dev(1 - p, c, z, 1 - s)
    above, below = dev(p, c, z + 1, s), dev(p, c, z - 1, s)
    low, high = z > 0, z < levels - 1
    first, last = wide == 0, wide == n_wide - 1
    primary, other = c == s, c != s
    jz, lz = z // span_levels, z % span_levels
    peers = (None, sib, acr, mix)

    pend = []

    def go(cond, copy):
        guarded(cond, copy.start)
        pend.append((cond, copy))

    def arrive(cond, view, sem):
        guarded(cond, remote(view, view, sem, sem, sib).wait_recv)

    barrier = pltpu.get_barrier_semaphore()

    def greet(peer):
        pl.semaphore_signal(barrier, inc=1, device_id=peer, device_id_type=MESH)

    for peer in (sib, acr, mix, bes, diag):
        greet(peer)
    pl.when(high)(lambda: greet(above))
    pl.when(low)(lambda: greet(below))
    far_next, far_prev = both(s == 1, high), both(s == 0, low)
    pl.when(far_next)(lambda: greet((dp, wide + 1)))
    pl.when(far_prev)(lambda: greet((dp, wide - 1)))
    count = 5 + jnp.where(high, 1, 0) + jnp.where(low, 1, 0)
    count = count + jnp.where(s == 1, jnp.where(high, 1, 0), jnp.where(low, 1, 0))

    def shard(level, side):
        return span((level * 2 + side) * rows, rows)

    def quart(k):
        return span(k * quarter, quarter)

    locals_ = [
        pltpu.make_async_copy(frames, fbuf.at[:, pl.ds(fr, fr)], loc.at[0]),
        pltpu.make_async_copy(conv_in, conv, loc.at[1]),
        pltpu.make_async_copy(embed_in, embed, loc.at[2]),
    ]
    locals_ += [
        pltpu.make_async_copy(in_w[m].at[:, quart(j)], weights.at[m, shard(z, s)], loc.at[3 + m]) for m in range(3)
    ]
    own_og = [pltpu.make_async_copy(og_in.at[g * 2 + c], og.at[0, g], loc.at[6 + g]) for g in range(2)]
    own_o = pltpu.make_async_copy(wo, out_w.at[0, shard(lz, s)], loc.at[8])
    at_source = j == jz
    for copy in locals_ + own_og:
        copy.start()
    pl.when(at_source)(own_o.start)

    def plan():
        shape = pick.shape
        lane_of = lax.broadcasted_iota(jnp.int32, shape, 1)
        limits = jnp.zeros(shape, jnp.int32)
        row_of = lax.broadcasted_iota(jnp.int32, klim.shape, 0)
        keys = jnp.zeros(klim.shape, jnp.int32)
        for g in range(2):
            for clip in range(clips):
                group = g * 2 + c
                bucket = clip_bucket[group, clip]
                owner = jnp.int32(0)
                for b in range(bucket_owner.shape[0]):
                    owner = owner + jnp.where(bucket == b, bucket_owner[b], 0)
                count_ = clip_grid[group, clip, 0] * clip_grid[group, clip, 1]
                keys = keys + jnp.where(row_of == g * clips + clip, jnp.where(count_ > 0, count_, sites), 0)
                for ab in range(4):
                    to = (1 - p if ab // 2 else p) * 2 + (1 - c if ab % 2 else c)
                    for f in range(fr):
                        hit = jnp.where(wide * fr + f < clip_frames[group, clip], count_, 0)
                        hit = jnp.where(owner == to, hit, 0)
                        limits = limits + jnp.where(lane_of == ((ab * 2 + g) * clips + clip) * fr + f, hit, 0)
        site = lax.broadcasted_iota(jnp.int32, shape, 0)
        pick[...] = jnp.where(site < limits, 1.0, 0.0).astype(BF16)
        key_of = lax.broadcasted_iota(jnp.int32, klim.shape, 1) % sites
        klim[...] = jnp.where(key_of < keys, 1.0, 0.0).astype(F32)

    @pl.when(first)
    def _():
        fbuf[:, 0:fr] = jnp.zeros((clips, fr, sites, channels), BF16)

    plan()
    pl.semaphore_wait(barrier, count)

    go(
        jnp.logical_not(last),
        remote(frames, fbuf.at[:, pl.ds(0, fr)], halo.at[0], halo.at[1], (dp, wide + 1)),
    )
    j_bes = 2 * (1 - s) + p
    for m in (0, 1, 3, 2):
        for piece in range(4):
            cols = pl.ds(piece * quarter, quarter)
            if m == 3:
                view = out_w.at[0, shard(lz, s), cols]
                go(both(primary, j_bes == jz), remote(wo.at[:, cols], view, xo.at[0, piece], xo.at[1, piece], bes))
        if m < 3:
            view = weights.at[m, shard(z, s)]
            go(primary, remote(in_w[m].at[:, quart(j_bes)], view, xw.at[0, m], xw.at[1, m], bes))

    def z_start(m):
        locals_[3 + m].wait()
        view = weights.at[m, shard(z, c)]
        arrive(other, view, xw.at[1, m])
        go(high, remote(view, view, zs.at[m, z, 0], zr.at[m, z], above))
        go(low, remote(view, view, zs.at[m, z, 1], zr.at[m, z], below))
        go(other, remote(view, view, bs.at[m, z], br.at[m, z], sib))

    def z_step(m, t):
        for down in range(2):
            valid = z + t <= levels - 1 if down else z >= t
            i = jnp.where(valid, z + t if down else z - t, z)
            view = weights.at[m, shard(i, c)]
            arrive(valid, view, zr.at[m, i])
            if t < levels - 1:
                peer = below if down else above
                go(both(valid, low if down else high), remote(view, view, zs.at[m, i, down], zr.at[m, i], peer))
            go(valid, remote(view, view, bs.at[m, i], br.at[m, i], sib))

    def z_done(m):
        for i in range(levels):
            arrive(jnp.logical_or(z != i, primary), weights.at[m, shard(i, 1 - c)], br.at[m, i])

    def o_view(q, i, side):
        return out_w.at[q, shard(i // 4, side), span((i % 4) * quarter, quarter)]

    def o_start(k):
        if k == 0:
            pl.when(at_source)(own_o.wait)
        for i in range(levels * k // 4, levels * (k + 1) // 4):
            here, view = z == j * span_levels + i // 4, o_view(0, i, c)
            arrive(both(here, other), view, xo.at[1, i % 4])
            go(both(here, high), remote(view, view, zs.at[3, i, 0], zr.at[3, i], above))
            go(both(here, low), remote(view, view, zs.at[3, i, 1], zr.at[3, i], below))
            go(here, remote(view, o_view(1, i, c), os_.at[i], or_.at[i], bes))
            go(both(here, other), remote(view, view, bs.at[3, i], br.at[3, i], sib))

    def o_step(i):
        source = j * span_levels + i // 4
        view, away = o_view(0, i, c), z != source
        arrive(away, view, zr.at[3, i])
        go(both(z > source, high), remote(view, view, zs.at[3, i, 0], zr.at[3, i], above))
        go(both(z < source, low), remote(view, view, zs.at[3, i, 1], zr.at[3, i], below))
        go(away, remote(view, o_view(1, i, c), os_.at[i], or_.at[i], bes))
        go(away, remote(view, view, bs.at[3, i], br.at[3, i], sib))

    def o_cross(i):
        view = o_view(1, i, c)
        arrive(None, view, or_.at[i])
        go(None, remote(view, view, ds.at[i], dr.at[i], sib))

    def o_done():
        for i in range(levels):
            source = j * span_levels + i // 4
            arrive(jnp.logical_or(z != source, primary), o_view(0, i, 1 - c), br.at[3, i])
            arrive(None, o_view(1, i, 1 - c), dr.at[i])

    def encode():
        arrive(jnp.logical_not(first), fbuf.at[:, pl.ds(0, fr)], halo.at[1])
        locals_[0].wait()
        locals_[1].wait()
        for clip in range(clips):
            raw = fbuf[clip].astype(F32)
            active = (raw / (1.0 + jnp.exp(-raw))).astype(BF16)
            acc = raw[fr:].reshape(pair, channels)
            for tap in range(3):
                moved = active[fr - tap : 2 * fr - tap].reshape(pair, channels)
                acc = acc + jnp.dot(moved, conv[tap], preferred_element_type=F32)
            enc[j, pl.ds(clip * pair, pair)] = acc.astype(BF16)
        for k, peer in enumerate((acr, bes, diag)):
            go(None, remote(enc.at[j], enc.at[j], es.at[k], er.at[k], peer))

    def embed_block(k):
        p_ = 1 - p if k in (1, 3) else p
        s_ = 1 - s if k in (2, 3) else s
        jb = 2 * s_ + p_
        if k:
            arrive(None, enc.at[jb], er.at[k - 1])
        else:
            locals_[2].wait()

        @pl.loop(0, own // pair)
        def _(i):
            at = span(i * pair, pair)
            token = jnp.dot(enc[jb, at], embed[...], preferred_element_type=F32).astype(BF16)
            if k < 2:
                tokens[span(p_ * own + i * pair, pair)] = token
            floats = token.astype(F32)
            center = floats - jnp.mean(floats, axis=-1, keepdims=True)
            spread = jnp.mean(center * center, axis=-1, keepdims=True)
            norm = (center * lax.rsqrt(spread + EPS)).astype(BF16)
            where = span(jb * own + i * pair, pair)
            normed[where] = norm
            turned = norm.T
            for k_ in range(n_wide):
                normed_t[k_ % 2, pl.ds(k_ // 2 * rows, rows), where] = turned[k_ * rows : (k_ + 1) * rows]

    def lane(ab, g, clip, f):
        return pick[:, pl.ds(((ab * 2 + g) * clips + clip) * fr + f, 1)]

    def og_send(g, f):
        for ab in range(1, 4):
            target = g * 2 + (1 - c if ab % 2 else c)
            go(None, remote(og_in.at[target, f], og.at[ab, g, f], gs.at[ab, g, f], gr.at[ab, g, f], peers[ab]))

    def slab_rows(side, g, size):
        return span((side * 2 + g) * own, size)

    def select(g, f):
        for ab in range(1, 4):
            arrive(None, og.at[ab, g, f], gr.at[ab, g, f])
        if f == 0:
            own_og[g].wait()
        for clip in range(clips):
            at = pl.ds(((g * clips + clip) * fr + f) * sites, sites)

            @pl.loop(0, 4)
            def _(k):
                cols = span(k * quarter, quarter)
                value = sum(og[ab, g, f, :, cols] * lane(ab, g, clip, f) for ab in range(4))
                upst[at, cols] = value

    def project(m):
        z_done(m)

        @pl.loop(0, 2)
        def _(i):
            at = span(i * 2 * own, 2 * own)
            qkv[m, at] = jnp.dot(normed[at], weights[m], preferred_element_type=F32).astype(BF16)

    def wide_dot(x, y):
        return lax.dot_general(x, y, (((1,), (1,)), ((), ())), preferred_element_type=F32)

    def tall_dot(x, y):
        return lax.dot_general(x, y, (((0,), (0,)), ((), ())), preferred_element_type=F32)

    def score(side, g):
        @pl.loop(g * clips, (g + 1) * clips)
        def _(k):
            b = side * 2 * clips + k
            at = span(b * pair, pair)
            frame_of = lax.broadcasted_iota(jnp.int32, (pair, pair), 0) // sites
            key_of = lax.broadcasted_iota(jnp.int32, (pair, pair), 1) // sites
            valid = jnp.logical_and(frame_of == key_of, klim[pl.ds(k, 1), :] > 0)
            for h in range(heads):
                lanes = pl.ds(h * HEAD_DIM, HEAD_DIM)
                scores = jnp.where(valid, wide_dot(qkv[0, at, lanes], qkv[1, at, lanes]) * scale, masked_score)
                top = jnp.exp(scores - jnp.max(scores, axis=-1, keepdims=True))
                probs[b, h] = top * (1.0 / jnp.sum(top, axis=-1, keepdims=True))

    def attend(side):
        @pl.loop(0, 2 * clips)
        def _(k):
            b = side * 2 * clips + k
            at = span(b * pair, pair)
            for h in range(heads):
                lanes = pl.ds(h * HEAD_DIM, HEAD_DIM)
                att[at, lanes] = jnp.dot(
                    probs[b, h].astype(BF16), qkv[2, at, lanes], preferred_element_type=F32
                ).astype(BF16)

    def att_send():
        at = slab_rows(1 - s, 0, 2 * own)
        go(None, remote(att.at[at], att_x, ps.at[0], pr.at[0], bes))

    def turn(q):
        if q:
            arrive(None, att_x, pr.at[0])

        @pl.loop(0, 2 * own // pair)
        def _(i):
            to = span(i * pair, pair)
            block = att_x[to] if q else att[span(s * 2 * own + i * pair, pair)]
            turned = block.T
            for k_ in range(2 * span_levels):
                att_t[q, k_ % 2, pl.ds(k_ // 2 * rows, rows), to] = turned[k_ * rows : (k_ + 1) * rows]

    def back_values(side):
        @pl.loop(0, 2 * clips)
        def _(k):
            b = side * 2 * clips + k
            at = span(b * pair, pair)
            for h in range(heads):
                lanes = pl.ds(h * HEAD_DIM, HEAD_DIM)
                dqkv[2, at, lanes] = tall_dot(probs[b, h].astype(BF16), datt[at, lanes]).astype(BF16)

    def attend_back(side, g):
        @pl.loop(g * clips, (g + 1) * clips)
        def _(k):
            b = side * 2 * clips + k
            at = span(b * pair, pair)
            for h in range(heads):
                lanes = pl.ds(h * HEAD_DIM, HEAD_DIM)
                q, k_, v, g = qkv[0, at, lanes], qkv[1, at, lanes], qkv[2, at, lanes], datt[at, lanes]
                prob = probs[b, h]
                d_probs = wide_dot(g, v)
                inner = jnp.sum(prob * d_probs, axis=-1, keepdims=True)
                d_scores = (prob * (d_probs - inner) * scale).astype(BF16)
                dqkv[0, at, lanes] = jnp.dot(d_scores, k_, preferred_element_type=F32).astype(BF16)
                dqkv[1, at, lanes] = tall_dot(d_scores, q).astype(BF16)

    def back_project(q, g):
        at, to = pl.ds(g * own, own), slab_rows(s, g, own)
        value = wide_dot(upst[at], out_w[q]).astype(BF16)
        if q:
            datt_x[at] = value
            go(None, remote(datt_x.at[at], datt.at[to], us.at[g], ur.at[g], bes))
        else:
            datt[to] = value

    def datt_done(g):
        arrive(None, datt.at[slab_rows(1 - s, g, own)], ur.at[g])

    def combine(g):
        keep_tokens = jnp.where(p == 0, 1.0, 0.0).astype(F32)
        at, to = slab_rows(s, g, own), pl.ds(g * own, own)

        @pl.loop(0, 4)
        def _(k):
            cols = span(k * quarter, quarter)
            value = jnp.dot(att[at], out_w[0, :, cols], preferred_element_type=F32)
            value = value + jnp.dot(att_x[to], out_w[1, :, cols], preferred_element_type=F32)
            comb[to, cols] = (value + tokens[to, cols].astype(F32) * keep_tokens).astype(BF16)

    def slots(g):
        for f in range(fr):
            for ab in (3, 2, 1, 0):
                slot = og.at[ab, g, f] if ab else y_in.at[0, g, f]

                @pl.loop(0, 4)
                def _(k):
                    cols = span(k * quarter, quarter)
                    slot[:, cols] = sum(
                        comb[pl.ds(((g * clips + clip) * fr + f) * sites, sites), cols] * lane(ab, g, clip, f)
                        for clip in range(clips)
                    )

                if ab:
                    go(None, remote(slot, y_in.at[ab, g, f], ys.at[ab, g, f], yr.at[ab, g, f], peers[ab]))

    def finish_out(g):
        for f in range(fr):
            for ab in range(1, 4):
                arrive(None, y_in.at[ab, g, f], yr.at[ab, g, f])
            for b in range(2):
                target = g * 2 + (1 - c if b else c)
                block_out[target, f] = (y_in[b, g, f].astype(F32) + y_in[2 + b, g, f].astype(F32)).astype(BF16)

    def message(m, i):
        return span(i * rows, rows)

    def terms(m, side, put):
        if m < 3:

            @pl.loop(0, 2)
            def _(i):
                at = span(i * (width // 4), width // 4)
                put(at, jnp.dot(normed_t[side, at], dqkv[m], preferred_element_type=F32))
        else:

            @pl.loop(0, 4)
            def _(piece):
                cols = span(piece * quarter, quarter)
                value = jnp.dot(att_t[m - 3, side], upst[:, cols], preferred_element_type=F32)
                for k in range(span_levels):
                    put(span((k * 4 + piece) * rows, rows), value[k * rows : (k + 1) * rows])

    def emit(m):
        def put(at, value):
            term_out[m, at] = value.astype(BF16)

        terms(m, 1 - c, put)
        go(None, remote(term_out.at[m], term_in.at[m], cs.at[m], cr.at[m], sib))

    def fold(m):
        arrive(None, term_in.at[m], cr.at[m])
        if m == 3:
            arrive(None, keep_x, ks.at[1])

        def put(at, value):
            value = value + term_in[m, at].astype(F32)
            if m == 3:
                value = value + keep_x[at].astype(F32)
            keep[m, at] = value.astype(BF16)

        terms(m, c, put)
        if m == 4:
            go(None, remote(keep.at[4], keep_x, ks.at[0], ks.at[1], bes))

    def target(m, i):
        return i if m < 3 else j * span_levels + i // 4

    def add_in(m, i, source, sem):
        at = message(m, i)
        arrive(None, source.at[m, at], sem.at[m, i])
        keep[m, at] = (keep[m, at].astype(F32) + source[m, at].astype(F32)).astype(BF16)

    def pass_on(m, *ks):
        for k in ks:
            for part in range(levels * k // 4, levels * (k + 1) // 4):
                pass_one(m, part)

    def pass_one(m, k):
        i = jnp.where(z < levels // 2, levels - 1 - k, k) if m < 3 else k
        d = target(m, i)
        upward, downward = z < d, z > d
        pl.when(both(upward, low))(lambda: add_in(m, i, from_low, rl))
        pl.when(both(downward, high))(lambda: add_in(m, i, from_high, rh))
        at = message(m, i)
        view = keep.at[m, at]
        go(upward, remote(view, from_low.at[m, at], rs.at[m, i], rl.at[m, i], above))
        go(downward, remote(view, from_high.at[m, at], rs.at[m, i], rh.at[m, i], below))

    def settle(m):
        fin = fins[m]
        if m < 3:
            pl.when(low)(lambda: add_in(m, z, from_low, rl))
            pl.when(high)(lambda: add_in(m, z, from_high, rh))
            view, place = keep.at[m, message(m, z)], fin.at[:, quart(j)]
            go(other, remote(view, place, a_s.at[m, 0], a_r.at[m, 0], bes))
            go(other, remote(view, place, a_s.at[m, 1], a_r.at[m, 1], diag))

            @pl.when(primary)
            def _():
                fin[:, quart(j)] = keep[m, message(m, z)]

            go(primary, remote(view, place, b_s.at[m, 0], b_r.at[m, 0], acr))
        else:
            for piece in range(4):
                i = lz * 4 + piece
                cols = pl.ds(piece * quarter, quarter)
                pl.when(both(at_source, low))(lambda: add_in(m, i, from_low, rl))
                pl.when(both(at_source, high))(lambda: add_in(m, i, from_high, rh))
                go(
                    both(at_source, other),
                    remote(keep.at[m, message(m, i)], fin.at[:, cols], a_s.at[m, piece], a_r.at[m, piece], bes),
                )

                @pl.when(both(at_source, primary))
                def _():
                    fin[:, cols] = keep[m, message(m, i)]

    def spread(m):
        fin = fins[m]
        if m == 3:
            p_z = jz % 2
            for piece in range(4):
                place = fin.at[:, pl.ds(piece * quarter, quarter)]
                arrive(both(primary, j_bes == jz), place, a_r.at[m, piece])
                go(both(primary, p == p_z), remote(place, place, b_s.at[m, piece], b_r.at[m, piece], acr))

    def share(m):
        fin = fins[m]
        if m < 3:
            arrive(primary, fin.at[:, quart(j_bes)], a_r.at[m, 0])
            arrive(primary, fin.at[:, quart(2 * (1 - s) + 1 - p)], a_r.at[m, 1])
            arrive(primary, fin.at[:, quart(2 * s + 1 - p)], b_r.at[m, 0])
        else:
            for piece in range(4):
                place = fin.at[:, pl.ds(piece * quarter, quarter)]
                arrive(both(primary, p != jz % 2), place, b_r.at[m, piece])
        go(primary, remote(fin, fin, f_s.at[m], f_r.at[m], sib))

    def complete(m):
        arrive(other, fins[m], f_r.at[m])

    pieces = [(g, f) for g in range(2) for f in range(fr)]
    steps = [(t, m) for t in range(1, levels) for m in range(2)]
    done = [0]

    def advance(k):
        while done[0] < len(steps) * k // 6:
            t, m = steps[done[0]]
            z_step(m, t)
            done[0] += 1

    def v_steps(k):
        for t in range(1 + (levels - 1) * k // 3, 1 + (levels - 1) * (k + 1) // 3):
            z_step(2, t)


    def o_steps(k):
        for i in range(levels * k // 4, levels * (k + 1) // 4):
            o_step(i)

    def o_crosses(k):
        for i in range(levels * k // 4, levels * (k + 1) // 4):
            o_cross(i)

    z_start(0)
    z_start(1)
    advance(1)
    encode()
    og_send(*pieces[0])
    og_send(*pieces[1])
    og_send(*pieces[2])
    og_send(*pieces[3])
    z_start(2)
    advance(2)
    o_start(0)
    embed_block(0)
    o_start(1)
    advance(3)
    o_start(2)
    embed_block(1)
    advance(4)
    o_start(3)
    embed_block(2)
    advance(5)
    embed_block(3)
    advance(6)
    project(0)
    o_steps(0)
    select(*pieces[0])
    project(1)
    o_steps(1)
    o_crosses(0)
    v_steps(0)
    select(*pieces[1])
    score(1 - s, 0)
    o_steps(2)
    o_crosses(1)
    score(1 - s, 1)
    o_steps(3)
    o_crosses(2)
    v_steps(1)
    score(s, 0)
    o_crosses(3)
    select(*pieces[2])
    o_done()
    back_project(1, 0)
    back_project(0, 0)
    score(s, 1)
    v_steps(2)
    project(2)
    attend(1 - s)
    select(*pieces[3])
    back_project(1, 1)
    att_send()
    back_project(0, 1)
    attend(s)
    back_values(s)
    attend_back(s, 0)
    attend_back(s, 1)
    turn(0)
    datt_done(0)
    datt_done(1)
    back_values(1 - s)
    attend_back(1 - s, 0)
    attend_back(1 - s, 1)
    emit(2)
    emit(1)
    fold(2)
    pass_on(2, 0)
    fold(1)
    turn(1)
    pass_on(2, 1)
    emit(4)
    pass_on(2, 2)
    fold(4)
    pass_on(2, 3)
    combine(0)
    pass_on(1, 0)
    slots(0)
    emit(0)
    pass_on(1, 1)
    emit(3)
    pass_on(1, 2)
    fold(0)
    pass_on(1, 3)
    settle(2)
    combine(1)
    fold(3)
    pass_on(3, 0, 1)
    slots(1)
    pass_on(3, 2, 3)
    settle(1)
    pass_on(0, 0, 1)
    share(2)
    settle(3)
    pass_on(0, 2, 3)
    spread(3)
    settle(0)
    share(1)
    share(3)
    finish_out(0)
    finish_out(1)
    share(0)
    for m in (3, 2, 1, 0):
        complete(m)
    for cond, copy in pend:
        guarded(cond, copy.wait_send)


def run_block(n_wide, frames, conv_w, embed_w, wq, wk, wv, wo, out_grad, *plan):
    clips, fr, sites, channels = frames.shape
    rows, width = wq.shape
    quarter, levels = width // 4, n_wide // 2
    own, pair = clips * fr * sites, fr * sites
    total = 4 * own
    heads = quarter // HEAD_DIM
    dma = pltpu.SemaphoreType.DMA
    anywhere = pl.BlockSpec(memory_space=pl.ANY)
    vmem = pl.BlockSpec(memory_space=pltpu.VMEM)

    def buf(*shape, dtype=BF16):
        return pltpu.VMEM(shape, dtype)

    reach = levels * rows
    scratch = [
        buf(clips, 2 * fr, sites, channels),
        buf(3, channels, channels),
        buf(channels, width),
        buf(3, width, quarter),
        buf(2, quarter, width),
        buf(4, own, channels),
        buf(2 * own, width),
        buf(total, width),
        buf(2, width // 2, total),
        buf(4, 2, fr, sites, width),
        buf(2 * own, width),
        buf(3, total, quarter),
        buf(total, quarter),
        buf(2 * own, quarter),
        buf(total, quarter),
        buf(2 * own, quarter),
        buf(2, 2, quarter // 2, 2 * own),
        buf(3, total, quarter),
        buf(total // pair, heads, pair, pair, dtype=F32),
        buf(2 * own, width),
        buf(4, 2, fr, sites, width),
        buf(5, reach, quarter),
        buf(5, reach, quarter),
        buf(5, reach, quarter),
        buf(reach, quarter),
        buf(4, reach, quarter),
        buf(4, reach, quarter),
        buf(sites, 8 * clips * fr),
        buf(2 * clips, pair, dtype=F32),
        dma((9,)),
        dma((2,)),
        dma((2, 3)),
        dma((2, 4)),
        dma((4, levels, 2)),
        dma((4, levels)),
        dma((4, levels)),
        dma((4, levels)),
        *([dma((levels,))] * 4),
        dma((3,)),
        dma((3,)),
        dma((4, 2, fr)),
        dma((4, 2, fr)),
        *([dma((2,))] * 4),
        dma((4, 2, fr)),
        dma((4, 2, fr)),
        dma((5,)),
        dma((5,)),
        dma((2,)),
        dma((4, levels)),
        dma((4, levels)),
        dma((4, levels)),
        *([dma((4, 4))] * 4),
        dma((4,)),
        dma((4,)),
    ]
    return pl.pallas_call(
        functools.partial(kernel, n_wide, clips, fr, sites, 1.0 / math.sqrt(HEAD_DIM)),
        out_shape=[jax.ShapeDtypeStruct(out_grad.shape, BF16)]
        + [jax.ShapeDtypeStruct((rows, width), BF16)] * 4,
        in_specs=[anywhere] * 8 + [pl.BlockSpec(memory_space=pltpu.SMEM)] * 4,
        out_specs=[vmem] * 5,
        scratch_shapes=scratch,
        compiler_params=pltpu.CompilerParams(
            collective_id=0, has_side_effects=True, vmem_limit_bytes=63 * 1024 * 1024
        ),
        cost_estimate=pl.CostEstimate(flops=12_000_000_000, bytes_accessed=20_000_000, transcendentals=0),
        name="section",
    )(frames, conv_w, embed_w, wq, wk, wv, wo, out_grad, *plan)


def body(
    frames,
    conv_weight,
    embed_weight,
    query_weight,
    key_weight,
    value_weight,
    output_weight,
    out_grad,
    bucket_owner,
    clip_bucket,
    clip_frames,
    clip_grid,
):
    n_wide = lax.axis_size("wide")
    block, grad_q, grad_k, grad_v, grad_o = run_block(
        n_wide,
        frames[0],
        conv_weight,
        embed_weight,
        query_weight,
        key_weight,
        value_weight,
        output_weight,
        out_grad[0],
        bucket_owner,
        clip_bucket,
        clip_frames,
        clip_grid,
    )
    return (block[None], *(g.astype(F32) for g in (grad_q, grad_k, grad_v, grad_o)))


def solution(mesh):
    rows = P("wide", None)
    slabs = P("dp", None, "wide", None, None)
    in_specs = (slabs, P(), P(), rows, rows, rows, rows, slabs, P(), P(), P(), P())
    out_specs = (slabs, rows, rows, rows, rows)
    return jax.shard_map(body, mesh=mesh, in_specs=in_specs, out_specs=out_specs, check_vma=False)
```

```python
import functools
import math

import jax
import jax.numpy as jnp
from jax import lax
from jax.experimental import pallas as pl
from jax.experimental.pallas import tpu as pltpu
from jax.sharding import PartitionSpec as P

HEAD_DIM = 128
MESH = pl.DeviceIdType.MESH
EPS = 1e-06
masked_score = -1e30
F32, BF16 = jnp.float32, jnp.bfloat16


def remote(src, dst, send, recv, peer):
    return pltpu.make_async_remote_copy(
        src_ref=src, dst_ref=dst, send_sem=send, recv_sem=recv, device_id=peer, device_id_type=MESH
    )


def span(start, size):
    return pl.ds(pl.multiple_of(start, 128 if size % 128 == 0 else 16), size)


def both(*conds):
    out = None
    for cond in conds:
        if cond is not None:
            out = cond if out is None else jnp.logical_and(out, cond)
    return out


def guarded(cond, action):
    if cond is None:
        action()
    else:
        pl.when(cond)(action)


def kernel(n_wide, clips, fr, sites, scale, *refs):
    frames, conv_in, embed_in, wq, wk, wv, wo, og_in, bucket_owner, clip_bucket, clip_frames, clip_grid = refs[:12]
    block_out, fin_q, fin_k, fin_v, fin_o = refs[12:17]
    (
        fbuf, conv, embed, weights, out_w, enc, tokens, normed, normed_t, og, upst, qkv, datt, datt_x, att, att_x,
        att_t, dqkv, probs, comb, y_in, term_out, term_in, keep, keep_x, from_low, from_high, pick, klim,
    ) = refs[17:46]
    (
        loc, halo, xw, xo, zs, zr, bs, br, os_, or_, ds, dr, es, er, gs, gr, us, ur, ps, pr, ys, yr, cs, cr, ks,
        rs, rl, rh, a_s, a_r, b_s, b_r, f_s, f_r,
    ) = refs[46:]
    levels = n_wide // 2
    in_w = (wq, wk, wv)
    fins = (fin_q, fin_k, fin_v, fin_o)
    rows, width = wq.shape
    quarter = width // 4
    span_levels = levels // 4
    own = clips * fr * sites
    pair = fr * sites
    total = 4 * own
    channels = embed_in.shape[0]
    heads = quarter // HEAD_DIM

    dp, wide = lax.axis_index("dp"), lax.axis_index("wide")
    p, c, z, s = dp // 2, dp % 2, wide // 2, wide % 2
    j = 2 * s + p

    def dev(p_, c_, z_, s_):
        return (p_ * 2 + c_, z_ * 2 + s_)

    sib, acr, mix = dev(p, 1 - c, z, s), dev(1 - p, c, z, s), dev(1 - p, 1 - c, z, s)
    bes, diag = dev(p, c, z, 1 - s), dev(1 - p, c, z, 1 - s)
    above, below = dev(p, c, z + 1, s), dev(p, c, z - 1, s)
    low, high = z > 0, z < levels - 1
    first, last = wide == 0, wide == n_wide - 1
    primary, other = c == s, c != s
    jz, lz = z // span_levels, z % span_levels
    peers = (None, sib, acr, mix)

    pend = []

    def go(cond, copy):
        guarded(cond, copy.start)
        pend.append((cond, copy))

    def arrive(cond, view, sem):
        guarded(cond, remote(view, view, sem, sem, sib).wait_recv)

    barrier = pltpu.get_barrier_semaphore()

    def greet(peer):
        pl.semaphore_signal(barrier, inc=1, device_id=peer, device_id_type=MESH)

    for peer in (sib, acr, mix, bes, diag):
        greet(peer)
    pl.when(high)(lambda: greet(above))
    pl.when(low)(lambda: greet(below))
    far_next, far_prev = both(s == 1, high), both(s == 0, low)
    pl.when(far_next)(lambda: greet((dp, wide + 1)))
    pl.when(far_prev)(lambda: greet((dp, wide - 1)))
    count = 5 + jnp.where(high, 1, 0) + jnp.where(low, 1, 0)
    count = count + jnp.where(s == 1, jnp.where(high, 1, 0), jnp.where(low, 1, 0))

    def shard(level, side):
        return span((level * 2 + side) * rows, rows)

    def quart(k):
        return span(k * quarter, quarter)

    locals_ = [
        pltpu.make_async_copy(frames, fbuf.at[:, pl.ds(fr, fr)], loc.at[0]),
        pltpu.make_async_copy(conv_in, conv, loc.at[1]),
        pltpu.make_async_copy(embed_in, embed, loc.at[2]),
    ]
    locals_ += [
        pltpu.make_async_copy(in_w[m].at[:, quart(j)], weights.at[m, shard(z, s)], loc.at[3 + m]) for m in range(3)
    ]
    own_og = [pltpu.make_async_copy(og_in.at[g * 2 + c], og.at[0, g], loc.at[6 + g]) for g in range(2)]
    own_o = pltpu.make_async_copy(wo, out_w.at[0, shard(lz, s)], loc.at[8])
    at_source = j == jz
    for copy in locals_ + own_og:
        copy.start()
    pl.when(at_source)(own_o.start)

    def plan():
        shape = pick.shape
        lane_of = lax.broadcasted_iota(jnp.int32, shape, 1)
        limits = jnp.zeros(shape, jnp.int32)
        row_of = lax.broadcasted_iota(jnp.int32, klim.shape, 0)
        keys = jnp.zeros(klim.shape, jnp.int32)
        for g in range(2):
            for clip in range(clips):
                group = g * 2 + c
                bucket = clip_bucket[group, clip]
                owner = jnp.int32(0)
                for b in range(bucket_owner.shape[0]):
                    owner = owner + jnp.where(bucket == b, bucket_owner[b], 0)
                count_ = clip_grid[group, clip, 0] * clip_grid[group, clip, 1]
                keys = keys + jnp.where(row_of == g * clips + clip, jnp.where(count_ > 0, count_, sites), 0)
                for ab in range(4):
                    to = (1 - p if ab // 2 else p) * 2 + (1 - c if ab % 2 else c)
                    for f in range(fr):
                        hit = jnp.where(wide * fr + f < clip_frames[group, clip], count_, 0)
                        hit = jnp.where(owner == to, hit, 0)
                        limits = limits + jnp.where(lane_of == ((ab * 2 + g) * clips + clip) * fr + f, hit, 0)
        site = lax.broadcasted_iota(jnp.int32, shape, 0)
        pick[...] = jnp.where(site < limits, 1.0, 0.0).astype(BF16)
        key_of = lax.broadcasted_iota(jnp.int32, klim.shape, 1) % sites
        klim[...] = jnp.where(key_of < keys, 1.0, 0.0).astype(F32)

    @pl.when(first)
    def _():
        fbuf[:, 0:fr] = jnp.zeros((clips, fr, sites, channels), BF16)

    plan()
    pl.semaphore_wait(barrier, count)

    go(
        jnp.logical_not(last),
        remote(frames, fbuf.at[:, pl.ds(0, fr)], halo.at[0], halo.at[1], (dp, wide + 1)),
    )
    j_bes = 2 * (1 - s) + p
    for m in (0, 1, 3, 2):
        for piece in range(4):
            cols = pl.ds(piece * quarter, quarter)
            if m == 3:
                view = out_w.at[0, shard(lz, s), cols]
                go(both(primary, j_bes == jz), remote(wo.at[:, cols], view, xo.at[0, piece], xo.at[1, piece], bes))
        if m < 3:
            view = weights.at[m, shard(z, s)]
            go(primary, remote(in_w[m].at[:, quart(j_bes)], view, xw.at[0, m], xw.at[1, m], bes))

    def z_start(m):
        locals_[3 + m].wait()
        view = weights.at[m, shard(z, c)]
        arrive(other, view, xw.at[1, m])
        go(high, remote(view, view, zs.at[m, z, 0], zr.at[m, z], above))
        go(low, remote(view, view, zs.at[m, z, 1], zr.at[m, z], below))
        go(other, remote(view, view, bs.at[m, z], br.at[m, z], sib))

    def z_step(m, t):
        for down in range(2):
            valid = z + t <= levels - 1 if down else z >= t
            i = jnp.where(valid, z + t if down else z - t, z)
            view = weights.at[m, shard(i, c)]
            arrive(valid, view, zr.at[m, i])
            if t < levels - 1:
                peer = below if down else above
                go(both(valid, low if down else high), remote(view, view, zs.at[m, i, down], zr.at[m, i], peer))
            go(valid, remote(view, view, bs.at[m, i], br.at[m, i], sib))

    def z_done(m):
        for i in range(levels):
            arrive(jnp.logical_or(z != i, primary), weights.at[m, shard(i, 1 - c)], br.at[m, i])

    def o_view(q, i, side):
        return out_w.at[q, shard(i // 4, side), span((i % 4) * quarter, quarter)]

    def o_start(k):
        if k == 0:
            pl.when(at_source)(own_o.wait)
        for i in range(levels * k // 4, levels * (k + 1) // 4):
            here, view = z == j * span_levels + i // 4, o_view(0, i, c)
            arrive(both(here, other), view, xo.at[1, i % 4])
            go(both(here, high), remote(view, view, zs.at[3, i, 0], zr.at[3, i], above))
            go(both(here, low), remote(view, view, zs.at[3, i, 1], zr.at[3, i], below))
            go(here, remote(view, o_view(1, i, c), os_.at[i], or_.at[i], bes))
            go(both(here, other), remote(view, view, bs.at[3, i], br.at[3, i], sib))

    def o_step(i):
        source = j * span_levels + i // 4
        view, away = o_view(0, i, c), z != source
        arrive(away, view, zr.at[3, i])
        go(both(z > source, high), remote(view, view, zs.at[3, i, 0], zr.at[3, i], above))
        go(both(z < source, low), remote(view, view, zs.at[3, i, 1], zr.at[3, i], below))
        go(away, remote(view, o_view(1, i, c), os_.at[i], or_.at[i], bes))
        go(away, remote(view, view, bs.at[3, i], br.at[3, i], sib))

    def o_cross(i):
        view = o_view(1, i, c)
        arrive(None, view, or_.at[i])
        go(None, remote(view, view, ds.at[i], dr.at[i], sib))

    def o_done():
        for i in range(levels):
            source = j * span_levels + i // 4
            arrive(jnp.logical_or(z != source, primary), o_view(0, i, 1 - c), br.at[3, i])
            arrive(None, o_view(1, i, 1 - c), dr.at[i])

    def encode():
        arrive(jnp.logical_not(first), fbuf.at[:, pl.ds(0, fr)], halo.at[1])
        locals_[0].wait()
        locals_[1].wait()
        for clip in range(clips):
            raw = fbuf[clip].astype(F32)
            active = (raw / (1.0 + jnp.exp(-raw))).astype(BF16)
            acc = raw[fr:].reshape(pair, channels)
            for tap in range(3):
                moved = active[fr - tap : 2 * fr - tap].reshape(pair, channels)
                acc = acc + jnp.dot(moved, conv[tap], preferred_element_type=F32)
            enc[j, pl.ds(clip * pair, pair)] = acc.astype(BF16)
        for k, peer in enumerate((acr, bes, diag)):
            go(None, remote(enc.at[j], enc.at[j], es.at[k], er.at[k], peer))

    def embed_block(k):
        p_ = 1 - p if k in (1, 3) else p
        s_ = 1 - s if k in (2, 3) else s
        jb = 2 * s_ + p_
        if k:
            arrive(None, enc.at[jb], er.at[k - 1])
        else:
            locals_[2].wait()

        @pl.loop(0, own // pair, unroll=2)
        def _(i):
            at = span(i * pair, pair)
            token = jnp.dot(enc[jb, at], embed[...], preferred_element_type=F32).astype(BF16)
            if k < 2:
                tokens[span(p_ * own + i * pair, pair)] = token
            floats = token.astype(F32)
            center = floats - jnp.mean(floats, axis=-1, keepdims=True)
            spread = jnp.mean(center * center, axis=-1, keepdims=True)
            norm = (center * lax.rsqrt(spread + EPS)).astype(BF16)
            where = span(jb * own + i * pair, pair)
            normed[where] = norm
            turned = norm.T
            for k_ in range(n_wide):
                normed_t[k_ % 2, pl.ds(k_ // 2 * rows, rows), where] = turned[k_ * rows : (k_ + 1) * rows]

    def lane(ab, g, clip, f):
        return pick[:, pl.ds(((ab * 2 + g) * clips + clip) * fr + f, 1)]

    def og_send(g, f):
        for ab in range(1, 4):
            target = g * 2 + (1 - c if ab % 2 else c)
            go(None, remote(og_in.at[target, f], og.at[ab, g, f], gs.at[ab, g, f], gr.at[ab, g, f], peers[ab]))

    def slab_rows(side, g, size):
        return span((side * 2 + g) * own, size)

    def select(g, f):
        for ab in range(1, 4):
            arrive(None, og.at[ab, g, f], gr.at[ab, g, f])
        if f == 0:
            own_og[g].wait()
        for clip in range(clips):
            at = pl.ds(((g * clips + clip) * fr + f) * sites, sites)

            @pl.loop(0, 4)
            def _(k):
                cols = span(k * quarter, quarter)
                value = sum(og[ab, g, f, :, cols] * lane(ab, g, clip, f) for ab in range(4))
                upst[at, cols] = value

    def project(m):
        z_done(m)

        @pl.loop(0, 2)
        def _(i):
            at = span(i * 2 * own, 2 * own)
            qkv[m, at] = jnp.dot(normed[at], weights[m], preferred_element_type=F32).astype(BF16)

    def wide_dot(x, y):
        return lax.dot_general(x, y, (((1,), (1,)), ((), ())), preferred_element_type=F32)

    def tall_dot(x, y):
        return lax.dot_general(x, y, (((0,), (0,)), ((), ())), preferred_element_type=F32)

    def score(side, g):
        @pl.loop(g * clips, (g + 1) * clips, unroll=2)
        def _(k):
            b = side * 2 * clips + k
            at = span(b * pair, pair)
            frame_of = lax.broadcasted_iota(jnp.int32, (pair, pair), 0) // sites
            key_of = lax.broadcasted_iota(jnp.int32, (pair, pair), 1) // sites
            valid = jnp.logical_and(frame_of == key_of, klim[pl.ds(k, 1), :] > 0)
            for h in range(heads):
                lanes = pl.ds(h * HEAD_DIM, HEAD_DIM)
                scores = jnp.where(valid, wide_dot(qkv[0, at, lanes], qkv[1, at, lanes]) * scale, masked_score)
                top = jnp.exp(scores - jnp.max(scores, axis=-1, keepdims=True))
                probs[b, h] = top * (1.0 / jnp.sum(top, axis=-1, keepdims=True))

    def attend(side):
        @pl.loop(0, 2 * clips, unroll=2)
        def _(k):
            b = side * 2 * clips + k
            at = span(b * pair, pair)
            for h in range(heads):
                lanes = pl.ds(h * HEAD_DIM, HEAD_DIM)
                att[at, lanes] = jnp.dot(
                    probs[b, h].astype(BF16), qkv[2, at, lanes], preferred_element_type=F32
                ).astype(BF16)

    def att_send():
        at = slab_rows(1 - s, 0, 2 * own)
        go(None, remote(att.at[at], att_x, ps.at[0], pr.at[0], bes))

    def turn(q):
        if q:
            arrive(None, att_x, pr.at[0])

        @pl.loop(0, 2 * own // pair)
        def _(i):
            to = span(i * pair, pair)
            block = att_x[to] if q else att[span(s * 2 * own + i * pair, pair)]
            turned = block.T
            for k_ in range(2 * span_levels):
                att_t[q, k_ % 2, pl.ds(k_ // 2 * rows, rows), to] = turned[k_ * rows : (k_ + 1) * rows]

    def back_values(side):
        @pl.loop(0, 2 * clips, unroll=2)
        def _(k):
            b = side * 2 * clips + k
            at = span(b * pair, pair)
            for h in range(heads):
                lanes = pl.ds(h * HEAD_DIM, HEAD_DIM)
                dqkv[2, at, lanes] = tall_dot(probs[b, h].astype(BF16), datt[at, lanes]).astype(BF16)

    def attend_back(side, g):
        @pl.loop(g * clips, (g + 1) * clips, unroll=2)
        def _(k):
            b = side * 2 * clips + k
            at = span(b * pair, pair)
            for h in range(heads):
                lanes = pl.ds(h * HEAD_DIM, HEAD_DIM)
                q, k_, v, g = qkv[0, at, lanes], qkv[1, at, lanes], qkv[2, at, lanes], datt[at, lanes]
                prob = probs[b, h]
                d_probs = wide_dot(g, v)
                inner = jnp.sum(prob * d_probs, axis=-1, keepdims=True)
                d_scores = (prob * (d_probs - inner) * scale).astype(BF16)
                dqkv[0, at, lanes] = jnp.dot(d_scores, k_, preferred_element_type=F32).astype(BF16)
                dqkv[1, at, lanes] = tall_dot(d_scores, q).astype(BF16)

    def back_project(q, g):
        at, to = pl.ds(g * own, own), slab_rows(s, g, own)
        value = wide_dot(upst[at], out_w[q]).astype(BF16)
        if q:
            datt_x[at] = value
            go(None, remote(datt_x.at[at], datt.at[to], us.at[g], ur.at[g], bes))
        else:
            datt[to] = value

    def datt_done(g):
        arrive(None, datt.at[slab_rows(1 - s, g, own)], ur.at[g])

    def combine(g):
        keep_tokens = jnp.where(p == 0, 1.0, 0.0).astype(F32)
        at, to = slab_rows(s, g, own), pl.ds(g * own, own)

        @pl.loop(0, 4)
        def _(k):
            cols = span(k * quarter, quarter)
            value = jnp.dot(att[at], out_w[0, :, cols], preferred_element_type=F32)
            value = value + jnp.dot(att_x[to], out_w[1, :, cols], preferred_element_type=F32)
            comb[to, cols] = (value + tokens[to, cols].astype(F32) * keep_tokens).astype(BF16)

    def slots(g):
        for f in range(fr):
            for ab in (3, 2, 1, 0):
                slot = og.at[ab, g, f] if ab else y_in.at[0, g, f]

                @pl.loop(0, 4)
                def _(k):
                    cols = span(k * quarter, quarter)
                    slot[:, cols] = sum(
                        comb[pl.ds(((g * clips + clip) * fr + f) * sites, sites), cols] * lane(ab, g, clip, f)
                        for clip in range(clips)
                    )

                if ab:
                    go(None, remote(slot, y_in.at[ab, g, f], ys.at[ab, g, f], yr.at[ab, g, f], peers[ab]))

    def finish_out(g):
        for f in range(fr):
            for ab in range(1, 4):
                arrive(None, y_in.at[ab, g, f], yr.at[ab, g, f])
            for b in range(2):
                target = g * 2 + (1 - c if b else c)
                block_out[target, f] = (y_in[b, g, f].astype(F32) + y_in[2 + b, g, f].astype(F32)).astype(BF16)

    def message(m, i):
        return span(i * rows, rows)

    def terms(m, side, put):
        if m < 3:

            @pl.loop(0, 2)
            def _(i):
                at = span(i * (width // 4), width // 4)
                put(at, jnp.dot(normed_t[side, at], dqkv[m], preferred_element_type=F32))
        else:

            @pl.loop(0, 4)
            def _(piece):
                cols = span(piece * quarter, quarter)
                value = jnp.dot(att_t[m - 3, side], upst[:, cols], preferred_element_type=F32)
                for k in range(span_levels):
                    put(span((k * 4 + piece) * rows, rows), value[k * rows : (k + 1) * rows])

    def emit(m):
        def put(at, value):
            term_out[m, at] = value.astype(BF16)

        terms(m, 1 - c, put)
        go(None, remote(term_out.at[m], term_in.at[m], cs.at[m], cr.at[m], sib))

    def fold(m):
        arrive(None, term_in.at[m], cr.at[m])
        if m == 3:
            arrive(None, keep_x, ks.at[1])

        def put(at, value):
            value = value + term_in[m, at].astype(F32)
            if m == 3:
                value = value + keep_x[at].astype(F32)
            keep[m, at] = value.astype(BF16)

        terms(m, c, put)
        if m == 4:
            go(None, remote(keep.at[4], keep_x, ks.at[0], ks.at[1], bes))

    def target(m, i):
        return i if m < 3 else j * span_levels + i // 4

    def add_in(m, i, source, sem):
        at = message(m, i)
        arrive(None, source.at[m, at], sem.at[m, i])
        keep[m, at] = (keep[m, at].astype(F32) + source[m, at].astype(F32)).astype(BF16)

    def pass_on(m, *ks):
        for k in ks:
            for part in range(levels * k // 4, levels * (k + 1) // 4):
                pass_one(m, part)

    def pass_one(m, k):
        i = jnp.where(z < levels // 2, levels - 1 - k, k) if m < 3 else k
        d = target(m, i)
        upward, downward = z < d, z > d
        pl.when(both(upward, low))(lambda: add_in(m, i, from_low, rl))
        pl.when(both(downward, high))(lambda: add_in(m, i, from_high, rh))
        at = message(m, i)
        view = keep.at[m, at]
        go(upward, remote(view, from_low.at[m, at], rs.at[m, i], rl.at[m, i], above))
        go(downward, remote(view, from_high.at[m, at], rs.at[m, i], rh.at[m, i], below))

    def settle(m):
        fin = fins[m]
        if m < 3:
            pl.when(low)(lambda: add_in(m, z, from_low, rl))
            pl.when(high)(lambda: add_in(m, z, from_high, rh))
            view, place = keep.at[m, message(m, z)], fin.at[:, quart(j)]
            go(other, remote(view, place, a_s.at[m, 0], a_r.at[m, 0], bes))
            go(other, remote(view, place, a_s.at[m, 1], a_r.at[m, 1], diag))

            @pl.when(primary)
            def _():
                fin[:, quart(j)] = keep[m, message(m, z)]

            go(primary, remote(view, place, b_s.at[m, 0], b_r.at[m, 0], acr))
        else:
            for piece in range(4):
                i = lz * 4 + piece
                cols = pl.ds(piece * quarter, quarter)
                pl.when(both(at_source, low))(lambda: add_in(m, i, from_low, rl))
                pl.when(both(at_source, high))(lambda: add_in(m, i, from_high, rh))
                go(
                    both(at_source, other),
                    remote(keep.at[m, message(m, i)], fin.at[:, cols], a_s.at[m, piece], a_r.at[m, piece], bes),
                )

                @pl.when(both(at_source, primary))
                def _():
                    fin[:, cols] = keep[m, message(m, i)]

    def spread(m):
        fin = fins[m]
        if m == 3:
            p_z = jz % 2
            for piece in range(4):
                place = fin.at[:, pl.ds(piece * quarter, quarter)]
                arrive(both(primary, j_bes == jz), place, a_r.at[m, piece])
                go(both(primary, p == p_z), remote(place, place, b_s.at[m, piece], b_r.at[m, piece], acr))

    def share(m):
        fin = fins[m]
        if m < 3:
            arrive(primary, fin.at[:, quart(j_bes)], a_r.at[m, 0])
            arrive(primary, fin.at[:, quart(2 * (1 - s) + 1 - p)], a_r.at[m, 1])
            arrive(primary, fin.at[:, quart(2 * s + 1 - p)], b_r.at[m, 0])
        else:
            for piece in range(4):
                place = fin.at[:, pl.ds(piece * quarter, quarter)]
                arrive(both(primary, p != jz % 2), place, b_r.at[m, piece])
        go(primary, remote(fin, fin, f_s.at[m], f_r.at[m], sib))

    def complete(m):
        arrive(other, fins[m], f_r.at[m])

    pieces = [(g, f) for g in range(2) for f in range(fr)]
    steps = [(t, m) for t in range(1, levels) for m in range(2)]
    done = [0]

    def advance(k):
        while done[0] < len(steps) * k // 6:
            t, m = steps[done[0]]
            z_step(m, t)
            done[0] += 1

    def v_steps(k):
        for t in range(1 + (levels - 1) * k // 3, 1 + (levels - 1) * (k + 1) // 3):
            z_step(2, t)


    def o_steps(k):
        for i in range(levels * k // 4, levels * (k + 1) // 4):
            o_step(i)

    def o_crosses(k):
        for i in range(levels * k // 4, levels * (k + 1) // 4):
            o_cross(i)

    z_start(0)
    z_start(1)
    advance(1)
    encode()
    og_send(*pieces[0])
    og_send(*pieces[1])
    og_send(*pieces[2])
    og_send(*pieces[3])
    z_start(2)
    advance(2)
    o_start(0)
    embed_block(0)
    o_start(1)
    advance(3)
    o_start(2)
    embed_block(1)
    advance(4)
    o_start(3)
    embed_block(2)
    advance(5)
    embed_block(3)
    advance(6)
    project(0)
    o_steps(0)
    select(*pieces[0])
    project(1)
    o_steps(1)
    o_crosses(0)
    v_steps(0)
    select(*pieces[1])
    score(1 - s, 0)
    o_steps(2)
    o_crosses(1)
    score(1 - s, 1)
    o_steps(3)
    o_crosses(2)
    v_steps(1)
    score(s, 0)
    o_crosses(3)
    select(*pieces[2])
    o_done()
    back_project(1, 0)
    back_project(0, 0)
    score(s, 1)
    v_steps(2)
    project(2)
    attend(1 - s)
    select(*pieces[3])
    back_project(1, 1)
    att_send()
    back_project(0, 1)
    attend(s)
    back_values(s)
    attend_back(s, 0)
    attend_back(s, 1)
    turn(0)
    datt_done(0)
    datt_done(1)
    back_values(1 - s)
    attend_back(1 - s, 0)
    attend_back(1 - s, 1)
    emit(2)
    emit(1)
    fold(2)
    pass_on(2, 0)
    fold(1)
    turn(1)
    pass_on(2, 1)
    emit(4)
    pass_on(2, 2)
    fold(4)
    pass_on(2, 3)
    combine(0)
    pass_on(1, 0)
    slots(0)
    emit(0)
    pass_on(1, 1)
    emit(3)
    pass_on(1, 2)
    fold(0)
    pass_on(1, 3)
    settle(2)
    combine(1)
    fold(3)
    pass_on(3, 0, 1)
    slots(1)
    pass_on(3, 2, 3)
    settle(1)
    pass_on(0, 0, 1)
    share(2)
    settle(3)
    pass_on(0, 2, 3)
    spread(3)
    settle(0)
    share(1)
    share(3)
    finish_out(0)
    finish_out(1)
    share(0)
    for m in (3, 2, 1, 0):
        complete(m)
    for cond, copy in pend:
        guarded(cond, copy.wait_send)


def run_block(n_wide, frames, conv_w, embed_w, wq, wk, wv, wo, out_grad, *plan):
    clips, fr, sites, channels = frames.shape
    rows, width = wq.shape
    quarter, levels = width // 4, n_wide // 2
    own, pair = clips * fr * sites, fr * sites
    total = 4 * own
    heads = quarter // HEAD_DIM
    dma = pltpu.SemaphoreType.DMA
    anywhere = pl.BlockSpec(memory_space=pl.ANY)
    vmem = pl.BlockSpec(memory_space=pltpu.VMEM)

    def buf(*shape, dtype=BF16):
        return pltpu.VMEM(shape, dtype)

    reach = levels * rows
    scratch = [
        buf(clips, 2 * fr, sites, channels),
        buf(3, channels, channels),
        buf(channels, width),
        buf(3, width, quarter),
        buf(2, quarter, width),
        buf(4, own, channels),
        buf(2 * own, width),
        buf(total, width),
        buf(2, width // 2, total),
        buf(4, 2, fr, sites, width),
        buf(2 * own, width),
        buf(3, total, quarter),
        buf(total, quarter),
        buf(2 * own, quarter),
        buf(total, quarter),
        buf(2 * own, quarter),
        buf(2, 2, quarter // 2, 2 * own),
        buf(3, total, quarter),
        buf(total // pair, heads, pair, pair, dtype=F32),
        buf(2 * own, width),
        buf(4, 2, fr, sites, width),
        buf(5, reach, quarter),
        buf(5, reach, quarter),
        buf(5, reach, quarter),
        buf(reach, quarter),
        buf(4, reach, quarter),
        buf(4, reach, quarter),
        buf(sites, 8 * clips * fr),
        buf(2 * clips, pair, dtype=F32),
        dma((9,)),
        dma((2,)),
        dma((2, 3)),
        dma((2, 4)),
        dma((4, levels, 2)),
        dma((4, levels)),
        dma((4, levels)),
        dma((4, levels)),
        *([dma((levels,))] * 4),
        dma((3,)),
        dma((3,)),
        dma((4, 2, fr)),
        dma((4, 2, fr)),
        *([dma((2,))] * 4),
        dma((4, 2, fr)),
        dma((4, 2, fr)),
        dma((5,)),
        dma((5,)),
        dma((2,)),
        dma((4, levels)),
        dma((4, levels)),
        dma((4, levels)),
        *([dma((4, 4))] * 4),
        dma((4,)),
        dma((4,)),
    ]
    return pl.pallas_call(
        functools.partial(kernel, n_wide, clips, fr, sites, 1.0 / math.sqrt(HEAD_DIM)),
        out_shape=[jax.ShapeDtypeStruct(out_grad.shape, BF16)]
        + [jax.ShapeDtypeStruct((rows, width), BF16)] * 4,
        in_specs=[anywhere] * 8 + [pl.BlockSpec(memory_space=pltpu.SMEM)] * 4,
        out_specs=[vmem] * 5,
        scratch_shapes=scratch,
        compiler_params=pltpu.CompilerParams(
            collective_id=0, has_side_effects=True, vmem_limit_bytes=63 * 1024 * 1024
        ),
        cost_estimate=pl.CostEstimate(flops=12_000_000_000, bytes_accessed=20_000_000, transcendentals=0),
        name="section",
    )(frames, conv_w, embed_w, wq, wk, wv, wo, out_grad, *plan)


def body(
    frames,
    conv_weight,
    embed_weight,
    query_weight,
    key_weight,
    value_weight,
    output_weight,
    out_grad,
    bucket_owner,
    clip_bucket,
    clip_frames,
    clip_grid,
):
    n_wide = lax.axis_size("wide")
    block, grad_q, grad_k, grad_v, grad_o = run_block(
        n_wide,
        frames[0],
        conv_weight,
        embed_weight,
        query_weight,
        key_weight,
        value_weight,
        output_weight,
        out_grad[0],
        bucket_owner,
        clip_bucket,
        clip_frames,
        clip_grid,
    )
    return (block[None], *(g.astype(F32) for g in (grad_q, grad_k, grad_v, grad_o)))


def solution(mesh):
    rows = P("wide", None)
    slabs = P("dp", None, "wide", None, None)
    in_specs = (slabs, P(), P(), rows, rows, rows, rows, slabs, P(), P(), P(), P())
    out_specs = (slabs, rows, rows, rows, rows)
    return jax.shard_map(body, mesh=mesh, in_specs=in_specs, out_specs=out_specs, check_vma=False)
```
